128 devices in a mesh: seq: 16 (over z, y), chan: 8 (over x, core).
Axes of the slice: x: 4, y: 4, z: 4, core: 2. Of those that a mesh axis runs over, the one named last changes fastest.
Arguments:
- tokens: bfloat16 [4096, 1024], P('seq', 'chan'), may hold values from -6 to 6
- in_proj: bfloat16 [1024, 3, 1024], P(None, None, 'chan'), may hold values from -0.1875 to 0.1875
- filter_one: float32 [4096, 1024], P('seq', 'chan'), may hold values from -0.09375 to 0.09375
- filter_two: float32 [4096, 1024], P('seq', 'chan'), may hold values from -0.09375 to 0.09375
- out_grad: float32 [4096, 1024], P('seq', 'chan'), may hold values from -0.75 to 0.75
Outputs:
- output: float32 [4096, 1024], P('seq', 'chan')
- token_grad: float32 [4096, 1024], P('seq', 'chan')
- proj_grad: float32 [1024, 3, 1024], P('seq', None, 'chan')
- filter_one_grad: float32 [4096, 1024], P('seq', 'chan')
- filter_two_grad: float32 [4096, 1024], P('seq', 'chan')
The draws below stay inside these ranges and needn't reach their ends.
All inputs are finite; a program needn't handle non-finite values.
Results may differ from the reference program's by a relative error of at most 0.0029.
Values may be sent and summed in bfloat16 or wider, within the bound.
A program may use at most 128 MiB of HBM per device.

```python
import jax
import jax.numpy as jnp

D = 1024
TOKENS = 4096


def spiked(entries, own_key, source, target, blocks, factor):
    def block_of(position):
        return (jnp.arange(entries.shape[position]) // (entries.shape[position] // blocks)).reshape((-1,) + (1,) * (entries.ndim - 1 - position))

    one_side = jax.random.permutation(own_key, blocks)[block_of(target)]
    second = (block_of(target) + blocks // 2) % blocks
    return jnp.where((block_of(source) == one_side) | (block_of(source) == second), factor * entries, entries)


def block_levels(own_key, shape, shards, low, high):
    gain, own = 1.0, jax.random.fold_in(own_key, 6)
    for axis_at, shards_of in shards:
        heights = jnp.exp(jax.random.uniform(jax.random.fold_in(own, axis_at), (shards_of,), jnp.float32, low / len(shards), high / len(shards)))
        gain = gain * jnp.repeat(heights, shape[axis_at] // shards_of).reshape([-1 if axis == axis_at else 1 for axis in range(len(shape))])
    return gain


def bell_draw(stream_key, shape, scale, reach, split=(), dtype=jnp.bfloat16):
    entries = scale * jax.random.normal(stream_key, shape, jnp.float32)
    if split:
        entries = entries * block_levels(stream_key, shape, split, -0.22, 0.18)
    return jnp.clip(entries, -reach, reach).astype(dtype)


def heavy_noise(own_key, extent, deviation, most, cuts, heavy, held_as=jnp.bfloat16):
    entries = deviation * jax.random.normal(own_key, extent, jnp.float32)
    if cuts:
        entries = entries * block_levels(own_key, extent, cuts, -0.22, 0.18)
    return jnp.clip(spiked(entries, jax.random.fold_in(own_key, 3), *heavy), -most, most).astype(held_as)


def setup_inputs(seed: int = 0) -> dict:
    arg_keys = jax.random.split(jax.random.key(seed), 6)
    tokens = heavy_noise(arg_keys[0], (TOKENS, D), 1.0, 6.0, ((0, 16), (1, 8)), (0, 1, 16, 2.0))
    in_proj = bell_draw(arg_keys[1], (D, 3, D), D ** -0.5, 0.1875, ((2, 8),))
    filter_one = bell_draw(arg_keys[2], (TOKENS, D), TOKENS ** -0.5, 0.09375, ((0, 16), (1, 8)), jnp.float32)
    filter_two = bell_draw(arg_keys[3], (TOKENS, D), TOKENS ** -0.5, 0.09375, ((0, 16), (1, 8)), jnp.float32)
    out_grad = bell_draw(arg_keys[4], (TOKENS, D), 0.125, 0.75, ((0, 16), (1, 8)), jnp.float32)
    return dict(tokens=tokens, in_proj=in_proj, filter_one=filter_one, filter_two=filter_two, out_grad=out_grad)


def spectrum_of(signal, length):
    return jnp.fft.rfft(signal, n=2 * length, axis=0)


def signal_of(spectrum, length):
    return jnp.fft.irfft(spectrum, n=2 * length, axis=0)[:length]


def reference(tokens, in_proj, filter_one, filter_two, out_grad):
    length = tokens.shape[0]
    width = tokens.shape[1]
    flat_proj = in_proj.reshape(width, 3 * width)
    projected = jnp.dot(tokens, flat_proj, preferred_element_type=jnp.float32).reshape(length, 3, width)
    values = projected[:, 0]
    gate_one = projected[:, 1]
    gate_two = projected[:, 2]
    spec_values = spectrum_of(values, length)
    spec_one = spectrum_of(filter_one, length)
    spec_two = spectrum_of(filter_two, length)
    mixed_one = signal_of(spec_one * spec_values, length)
    inner = gate_one * mixed_one
    spec_inner = spectrum_of(inner, length)
    mixed_two = signal_of(spec_two * spec_inner, length)
    output = gate_two * mixed_two
    grad_two = out_grad * gate_two
    grad_gate_two = out_grad * mixed_two
    spec_grad_two = spectrum_of(grad_two, length)
    grad_inner = signal_of(spec_grad_two * jnp.conj(spec_two), length)
    filter_two_grad = signal_of(spec_grad_two * jnp.conj(spec_inner), length)
    grad_one = grad_inner * gate_one
    grad_gate_one = grad_inner * mixed_one
    spec_grad_one = spectrum_of(grad_one, length)
    grad_values = signal_of(spec_grad_one * jnp.conj(spec_one), length)
    filter_one_grad = signal_of(spec_grad_one * jnp.conj(spec_values), length)
    grad_projected = jnp.stack([grad_values, grad_gate_one, grad_gate_two], axis=1).astype(jnp.bfloat16)
    flat_grad = grad_projected.reshape(length, 3 * width)
    token_grad = jnp.dot(flat_grad, flat_proj.T, preferred_element_type=jnp.float32)
    proj_grad = jnp.dot(tokens.T, flat_grad, preferred_element_type=jnp.float32).reshape(width, 3, width)
    return (output, token_grad, proj_grad, filter_one_grad, filter_two_grad)
```

```python
import functools

import jax
import jax.numpy as jnp
import numpy as np
from jax import lax
from jax.experimental import pallas as pl
from jax.experimental.pallas import tpu as pltpu
from jax.sharding import PartitionSpec as P

OUTER = 32
INNER = 128
LENGTH = OUTER * INNER
CH = 8
ROWS = OUTER * CH
BF16 = jnp.bfloat16
F32 = jnp.float32


def split_const(matrix):
    high = matrix.astype(np.float32).astype(BF16)
    low = (matrix - high.astype(np.float64)).astype(np.float32).astype(BF16)
    return high, low


def tables():
    outer = np.arange(OUTER)
    inner = np.arange(INNER)
    shifted = outer + 0.25
    theta = 2 * np.pi * np.outer(shifted, outer) / OUTER
    eye = np.eye(CH)
    forward = np.concatenate([np.kron(np.cos(theta), eye), np.kron(-np.sin(theta), eye)], axis=0)
    backward = np.concatenate([np.kron(np.cos(theta.T), eye), np.kron(-np.sin(theta.T), eye)], axis=1) / LENGTH
    psi = 2 * np.pi * (np.outer(inner, inner) % INNER) / INNER
    cos, sin = np.cos(psi), np.sin(psi)
    dft = np.block([[cos, -sin], [sin, cos]])
    idft = np.block([[cos, sin], [-sin, cos]])
    phi = np.repeat(2 * np.pi * np.outer(shifted, inner) / LENGTH, CH, axis=0)
    high, low = split_const(forward)
    fwd = np.concatenate([high, low, high], axis=1)
    high, low = split_const(backward)
    bwd = np.concatenate([high, low, high], axis=1)
    high, low = split_const(dft)
    dft3 = np.concatenate([high, low, high], axis=0)
    high, low = split_const(idft)
    idft3 = np.concatenate([high, low, high], axis=0)
    twiddle = np.stack([np.cos(phi), np.sin(phi)]).astype(np.float32)
    return fwd, bwd, dft3, idft3, twiddle


def halves(value):
    high = value.astype(BF16)
    low = (value - high.astype(F32)).astype(BF16)
    return high, low


def product(left, right):
    return jnp.dot(left, right, preferred_element_type=F32)


def to_spectra(signals, fwd_ref, dft_ref, cos, sin):
    high, low = halves(jnp.concatenate(signals, axis=1))
    stage = product(fwd_ref[...], jnp.concatenate([high, high, low], axis=0))
    rows = []
    for n in range(len(signals)):
        real = stage[:ROWS, n * INNER : (n + 1) * INNER]
        imag = stage[ROWS:, n * INNER : (n + 1) * INNER]
        rows.append(jnp.concatenate([real * cos + imag * sin, imag * cos - real * sin], axis=1))
    high, low = halves(jnp.concatenate(rows, axis=0))
    out = product(jnp.concatenate([high, high, low], axis=1), dft_ref[...])
    return [
        (out[n * ROWS : (n + 1) * ROWS, :INNER], out[n * ROWS : (n + 1) * ROWS, INNER:])
        for n in range(len(signals))
    ]


def to_signals(spectra, bwd_ref, idft_ref, cos, sin):
    stacked = jnp.concatenate([jnp.concatenate(pair, axis=1) for pair in spectra], axis=0)
    high, low = halves(stacked)
    out = product(jnp.concatenate([high, high, low], axis=1), idft_ref[...])
    columns = []
    for n in range(len(spectra)):
        real = out[n * ROWS : (n + 1) * ROWS, :INNER]
        imag = out[n * ROWS : (n + 1) * ROWS, INNER:]
        columns.append(jnp.concatenate([real * cos - imag * sin, imag * cos + real * sin], axis=0))
    high, low = halves(jnp.concatenate(columns, axis=1))
    signals = product(bwd_ref[...], jnp.concatenate([high, high, low], axis=0))
    return [signals[:, n * INNER : (n + 1) * INNER] for n in range(len(spectra))]


def times(first, second):
    return first[0] * second[0] - first[1] * second[1], first[0] * second[1] + first[1] * second[0]


def times_conj(first, second):
    return first[0] * second[0] + first[1] * second[1], first[1] * second[0] - first[0] * second[1]


def local_kernel(sig_ref, fwd_ref, bwd_ref, dft_ref, idft_ref, twiddle_ref, out_ref, grad_ref):
    cos, sin = twiddle_ref[0], twiddle_ref[1]
    values, gate_one, gate_two, filter_one, filter_two, out_grad = [sig_ref[n] for n in range(6)]
    grad_two = out_grad * gate_two
    spec_values, spec_one, spec_two, spec_grad_two = to_spectra(
        [values, filter_one, filter_two, grad_two], fwd_ref, dft_ref, cos, sin
    )
    mixed_one, grad_inner = to_signals(
        [times(spec_one, spec_values), times_conj(spec_grad_two, spec_two)], bwd_ref, idft_ref, cos, sin
    )
    inner = gate_one * mixed_one
    grad_one = grad_inner * gate_one
    spec_inner, spec_grad_one = to_spectra([inner, grad_one], fwd_ref, dft_ref, cos, sin)
    mixed_two, filter_two_grad, grad_values, filter_one_grad = to_signals(
        [
            times(spec_two, spec_inner),
            times_conj(spec_grad_two, spec_inner),
            times_conj(spec_grad_one, spec_one),
            times_conj(spec_grad_one, spec_values),
        ],
        bwd_ref,
        idft_ref,
        cos,
        sin,
    )
    out_ref[0] = gate_two * mixed_two
    out_ref[1] = filter_one_grad
    out_ref[2] = filter_two_grad
    grad_ref[0] = grad_values.astype(BF16)
    grad_ref[1] = (grad_inner * mixed_one).astype(BF16)
    grad_ref[2] = (out_grad * mixed_two).astype(BF16)


def local_part(signals):
    vmem = pl.BlockSpec(memory_space=pltpu.VMEM)
    return pl.pallas_call(
        local_kernel,
        out_shape=(
            jax.ShapeDtypeStruct((3, ROWS, INNER), F32),
            jax.ShapeDtypeStruct((3, ROWS, INNER), BF16),
        ),
        in_specs=[vmem] * 6,
        out_specs=(vmem, vmem),
        name="local_chain",
    )(signals, *[jnp.asarray(t) for t in tables()])


def shards(tokens, in_proj, filter_one, filter_two, out_grad):
    seq = lax.axis_size("seq")
    rows, width = tokens.shape
    full_tokens = lax.all_gather(tokens, "chan", axis=1, tiled=True)
    projected = jnp.einsum("rd,djc->jrc", full_tokens, in_proj, preferred_element_type=F32)
    stacked = jnp.concatenate([projected, jnp.stack([filter_one, filter_two, out_grad])], axis=0)
    blocks = stacked.reshape(6, rows, seq, CH).transpose(2, 0, 3, 1).reshape(seq, 6, CH, rows // INNER, INNER)
    arrived = lax.all_to_all(blocks.transpose(0, 1, 3, 2, 4), "seq", 0, 0)
    signals = arrived.transpose(1, 0, 2, 3, 4).reshape(6, ROWS, INNER)
    outs, grads = local_part(signals)

    def back(array):
        parted = array.reshape(3, seq, rows // INNER, CH, INNER).transpose(1, 0, 2, 3, 4)
        home = lax.all_to_all(parted, "seq", 0, 0)
        return home.transpose(1, 2, 4, 0, 3).reshape(3, rows, width)

    outs = back(outs)
    grads = back(grads)
    token_terms = jnp.einsum("jrc,djc->rd", grads, in_proj, preferred_element_type=F32)
    token_grad = lax.psum_scatter(token_terms, "chan", scatter_dimension=1, tiled=True)
    proj_grad = lax.psum_scatter(
        jnp.einsum("rd,jrc->djc", full_tokens, grads, preferred_element_type=F32),
        "seq",
        scatter_dimension=0,
        tiled=True,
    )
    return outs[0], token_grad, proj_grad, outs[1], outs[2]


def solution(mesh):
    in_specs = (
        P("seq", "chan"),
        P(None, None, "chan"),
        P("seq", "chan"),
        P("seq", "chan"),
        P("seq", "chan"),
    )
    out_specs = (
        P("seq", "chan"),
        P("seq", "chan"),
        P("seq", None, "chan"),
        P("seq", "chan"),
        P("seq", "chan"),
    )
    return jax.shard_map(shards, mesh=mesh, in_specs=in_specs, out_specs=out_specs, check_vma=False)
```

```python
import functools

import jax
import jax.numpy as jnp
import numpy as np
from jax import lax
from jax.experimental import pallas as pl
from jax.experimental.pallas import tpu as pltpu
from jax.sharding import PartitionSpec as P

OUTER = 32
INNER = 128
LENGTH = OUTER * INNER
CH = 8
ROWS = OUTER * CH
BF16 = jnp.bfloat16
F32 = jnp.float32


def split_const(matrix):
    high = matrix.astype(np.float32).astype(BF16)
    low = (matrix - high.astype(np.float64)).astype(np.float32).astype(BF16)
    return high, low


def tables():
    outer = np.arange(OUTER)
    inner = np.arange(INNER)
    shifted = outer + 0.25
    theta = 2 * np.pi * np.outer(shifted, outer) / OUTER
    eye = np.eye(CH)
    forward = np.concatenate([np.kron(np.cos(theta), eye), np.kron(-np.sin(theta), eye)], axis=0)
    backward = np.concatenate([np.kron(np.cos(theta.T), eye), np.kron(-np.sin(theta.T), eye)], axis=1) / LENGTH
    psi = 2 * np.pi * (np.outer(inner, inner) % INNER) / INNER
    cos, sin = np.cos(psi), np.sin(psi)
    dft = np.block([[cos, -sin], [sin, cos]])
    idft = np.block([[cos, sin], [-sin, cos]])
    phi = np.repeat(2 * np.pi * np.outer(shifted, inner) / LENGTH, CH, axis=0)
    fwd = np.concatenate(split_const(forward), axis=1)
    bwd = np.concatenate(split_const(backward), axis=1)
    dft2 = np.concatenate(split_const(dft), axis=0)
    idft2 = np.concatenate(split_const(idft), axis=0)
    twiddle = np.stack([np.cos(phi), np.sin(phi)]).astype(np.float32)
    return fwd, bwd, dft2, idft2, twiddle


def halves(value):
    high = value.astype(BF16)
    low = (value - high.astype(F32)).astype(BF16)
    return high, low


def product(left, right):
    return jnp.dot(left, right, preferred_element_type=F32)


def thrice(table, axis):
    high, low = jnp.split(table, 2, axis=axis)
    return jnp.concatenate([high, low, high], axis=axis)


def to_spectra(signals, fwd_ref, dft_ref, cos, sin):
    high, low = halves(jnp.concatenate(signals, axis=1))
    stage = product(thrice(fwd_ref[...], 1), jnp.concatenate([high, high, low], axis=0))
    rows = []
    for n in range(len(signals)):
        real = stage[:ROWS, n * INNER : (n + 1) * INNER]
        imag = stage[ROWS:, n * INNER : (n + 1) * INNER]
        rows.append(jnp.concatenate([real * cos + imag * sin, imag * cos - real * sin], axis=1))
    high, low = halves(jnp.concatenate(rows, axis=0))
    out = product(jnp.concatenate([high, high, low], axis=1), thrice(dft_ref[...], 0))
    return [
        (out[n * ROWS : (n + 1) * ROWS, :INNER], out[n * ROWS : (n + 1) * ROWS, INNER:])
        for n in range(len(signals))
    ]


def to_signals(spectra, bwd_ref, idft_ref, cos, sin):
    stacked = jnp.concatenate([jnp.concatenate(pair, axis=1) for pair in spectra], axis=0)
    high, low = halves(stacked)
    out = product(jnp.concatenate([high, high, low], axis=1), thrice(idft_ref[...], 0))
    columns = []
    for n in range(len(spectra)):
        real = out[n * ROWS : (n + 1) * ROWS, :INNER]
        imag = out[n * ROWS : (n + 1) * ROWS, INNER:]
        columns.append(jnp.concatenate([real * cos - imag * sin, imag * cos + real * sin], axis=0))
    high, low = halves(jnp.concatenate(columns, axis=1))
    signals = product(thrice(bwd_ref[...], 1), jnp.concatenate([high, high, low], axis=0))
    return [signals[:, n * INNER : (n + 1) * INNER] for n in range(len(spectra))]


def times(first, second):
    return first[0] * second[0] - first[1] * second[1], first[0] * second[1] + first[1] * second[0]


def times_conj(first, second):
    return first[0] * second[0] + first[1] * second[1], first[1] * second[0] - first[0] * second[1]


SEQ = 16
CHAN = 8
RING = 4
MESH = pl.DeviceIdType.MESH


def to_blocks(array):
    return [array[n * INNER : (n + 1) * INNER, :].T.reshape(SEQ, CH, INNER) for n in range(2)]


def chain_kernel(
    tok_hbm, w_hbm, one_hbm, two_hbm, grad_hbm, fwd_hbm, bwd_hbm, dft_hbm, idft_hbm, twiddle_hbm,
    sig_out, token_out, proj_out,
    tok, weights, local, fwd, bwd, dft, idft, twiddle, tok_t,
    send_a, recv_a, send_b, recv_b, send_g, recv_g, send_f, send_t, send_p,
    load_sem, tok_send, tok_recv, a_send, a_recv, b_send, b_recv, g_send, g_recv, f_send, f_recv,
    t_send, t_recv, p_send, p_recv, own_sem,
):
    me = lax.axis_index("seq")
    chan = lax.axis_index("chan")
    core = lax.rem(chan, 2)
    chip = lax.div(chan, 2)
    plane = lax.div(me, RING)
    row = lax.rem(me, RING)

    loads = [
        pltpu.make_async_copy(source, target, load_sem.at[n])
        for n, (source, target) in enumerate(
            [
                (tok_hbm, tok.at[chan]),
                (one_hbm, local.at[0]),
                (two_hbm, local.at[1]),
                (grad_hbm, local.at[2]),
                (w_hbm, weights),
                (fwd_hbm, fwd),
                (dft_hbm, dft),
                (twiddle_hbm, twiddle),
                (bwd_hbm, bwd),
                (idft_hbm, idft),
            ]
        )
    ]
    for load in loads:
        load.start()

    barrier = pltpu.get_barrier_semaphore()

    def greet_seq(k, carry):
        pl.semaphore_signal(
            barrier, inc=1, device_id=(lax.rem(me + k, SEQ), chan), device_id_type=MESH
        )
        return carry

    def greet_chan(k, carry):
        pl.semaphore_signal(
            barrier, inc=1, device_id=(me, lax.rem(chan + k, CHAN)), device_id_type=MESH
        )
        return carry

    lax.fori_loop(1, CHAN, greet_chan, 0)
    lax.fori_loop(1, SEQ, greet_seq, 0)
    pl.semaphore_wait(barrier, SEQ + CHAN - 2)

    def token_copy(source, slot, send, target):
        return pltpu.make_async_remote_copy(
            src_ref=source,
            dst_ref=tok.at[slot],
            send_sem=tok_send.at[send],
            recv_sem=tok_recv.at[slot],
            device_id=(me, target),
            device_id_type=MESH,
        )

    def across(k):
        return lax.rem(chip + k, RING) * 2 + core

    sibling = chip * 2 + (1 - core)
    own_sends = [token_copy(tok_hbm, chan, k, across(k)) for k in (2, 1, 3)]
    own_sends.append(token_copy(tok_hbm, chan, 0, sibling))
    for copy in own_sends:
        copy.start()

    def exchange(send, recv, send_sem, recv_sem):
        def copy(target, slot):
            return pltpu.make_async_remote_copy(
                src_ref=send.at[target],
                dst_ref=recv.at[slot],
                send_sem=send_sem.at[target],
                recv_sem=recv_sem.at[slot],
                device_id=(target, chan),
                device_id_type=MESH,
            )

        def start(k, carry):
            copy(lax.rem(me + k, SEQ), me).start()
            return carry

        def wait_recv(k, carry):
            source = lax.rem(me + SEQ - k, SEQ)
            copy(source, source).wait_recv()
            return carry

        def wait_send(k, carry):
            target = lax.rem(me + k, SEQ)
            copy(target, me).wait_send()
            return carry

        return tuple(
            functools.partial(lax.fori_loop, 1, SEQ, step, 0) for step in (start, wait_recv, wait_send)
        )

    a_start, a_arrive, a_leave = exchange(send_a, recv_a, a_send, a_recv)
    b_start, b_arrive, b_leave = exchange(send_b, recv_b, b_send, b_recv)
    g_start, g_arrive, g_leave = exchange(send_g, recv_g, g_send, g_recv)
    f_start, f_arrive, f_leave = exchange(send_f, sig_out, f_send, f_recv)

    for n in range(3):
        loads[1 + n].wait()
    for n in range(3):
        for half, block in enumerate(to_blocks(local[n])):
            send_a[:, n, half * CH : (half + 1) * CH, :] = block
    a_start()
    recv_a[me] = send_a[me]

    loads[0].wait()
    loads[4].wait()
    relays = []
    for n, k in enumerate((1, 3, 2)):
        slot = lax.rem(chip + RING - k, RING) * 2 + core
        token_copy(tok.at[slot], slot, 4 + n, sibling).wait_recv()
        relay = token_copy(tok.at[slot], slot, 4 + n, sibling)
        relay.start()
        relays.append(relay)
    for k in range(RING):
        slot = lax.rem(chip + k, RING) * 2 + (1 - core)
        token_copy(tok.at[slot], slot, 0, sibling).wait_recv()

    full = jnp.concatenate([tok[k] for k in range(CHAN)], axis=1)
    w_flat = jnp.concatenate([weights[j] for j in range(3)], axis=1)
    projected = product(full, w_flat)
    for n in range(3):
        for half, block in enumerate(to_blocks(projected[:, n * INNER : (n + 1) * INNER])):
            send_b[:, n, half * CH : (half + 1) * CH, :] = block
    b_start()
    recv_b[me] = send_b[me]

    for k in range(CHAN):
        tok_t[k * INNER : (k + 1) * INNER, :] = tok[k].T
    for n in range(5, 10):
        loads[n].wait()
    a_arrive()
    cos, sin = twiddle[0], twiddle[1]
    filter_one, filter_two, out_grad = [recv_a[:, n].reshape(ROWS, INNER) for n in range(3)]
    spec_one, spec_two = to_spectra([filter_one, filter_two], fwd, dft, cos, sin)

    b_arrive()
    values, gate_one, gate_two = [recv_b[:, n].reshape(ROWS, INNER) for n in range(3)]
    grad_two = out_grad * gate_two
    spec_values, spec_grad_two = to_spectra([values, grad_two], fwd, dft, cos, sin)
    mixed_one, grad_inner = to_signals(
        [times(spec_one, spec_values), times_conj(spec_grad_two, spec_two)], bwd, idft, cos, sin
    )
    inner = gate_one * mixed_one
    grad_one = grad_inner * gate_one
    spec_inner, spec_grad_one = to_spectra([inner, grad_one], fwd, dft, cos, sin)
    mixed_two, grad_values = to_signals(
        [times(spec_two, spec_inner), times_conj(spec_grad_one, spec_one)], bwd, idft, cos, sin
    )
    for n, grad in enumerate((grad_values, grad_inner * mixed_one, out_grad * mixed_two)):
        send_g[:, n] = grad.astype(BF16).reshape(SEQ, 2 * CH, INNER)
    g_start()
    recv_g[me] = send_g[me]
    filter_two_grad, filter_one_grad = to_signals(
        [times_conj(spec_grad_two, spec_inner), times_conj(spec_grad_one, spec_values)], bwd, idft, cos, sin
    )
    for n, signal in enumerate((gate_two * mixed_two, filter_one_grad, filter_two_grad)):
        send_f[:, n] = signal.reshape(SEQ, 2 * CH, INNER)
    f_start()
    own_f = pltpu.make_async_copy(send_f.at[me], sig_out.at[me], own_sem.at[0])
    own_f.start()

    g_arrive()
    columns = []
    for n in range(3):
        arrived = recv_g[:, n].astype(F32)
        columns.append(
            jnp.concatenate(
                [
                    arrived[:, half * CH : (half + 1) * CH, :].reshape(INNER, INNER).T.astype(BF16)
                    for half in range(2)
                ],
                axis=0,
            )
        )
    grads = jnp.concatenate(columns, axis=1)

    def proj_copy(target, slot):
        return pltpu.make_async_remote_copy(
            src_ref=send_p.at[target],
            dst_ref=proj_out.at[slot],
            send_sem=p_send.at[target],
            recv_sem=p_recv.at[slot],
            device_id=(target, chan),
            device_id_type=MESH,
        )

    def term_copy(target, slot):
        return pltpu.make_async_remote_copy(
            src_ref=send_t.at[target],
            dst_ref=token_out.at[slot],
            send_sem=t_send.at[target],
            recv_sem=t_recv.at[slot],
            device_id=(me, target),
            device_id_type=MESH,
        )

    depth = 1024 // SEQ
    for step in (2, 1, 3, 4):
        base = lax.rem(plane + step, RING) * RING
        slab = product(tok_t[pl.ds(pl.multiple_of(base * depth, 256), 256), :], grads).astype(BF16)
        for n in range(RING):
            for j in range(3):
                send_p[base + n, j] = slab[n * depth : (n + 1) * depth, j * INNER : (j + 1) * INNER]
        for n in (2, 1, 3, 0):
            if step < 4 or n > 0:
                proj_copy(base + lax.rem(row + n, RING), me).start()
        base = lax.rem(chip + step, RING) * 2
        columns = pl.ds(pl.multiple_of(base * INNER, 256), 256)
        w_rows = jnp.concatenate([weights[j, columns, :] for j in range(3)], axis=1)
        terms = lax.dot_general(grads, w_rows, (((1,), (1,)), ((), ())), preferred_element_type=F32)
        for n in range(2):
            send_t[base + n] = terms[:, n * INNER : (n + 1) * INNER].astype(BF16)
        if step < 4:
            term_copy(base + core, chan).start()
        term_copy(base + (1 - core), chan).start()
    own_p = pltpu.make_async_copy(send_p.at[me], proj_out.at[me], own_sem.at[1])
    own_p.start()
    own_t = pltpu.make_async_copy(send_t.at[chan], token_out.at[chan], own_sem.at[2])
    own_t.start()

    for copy in own_sends + relays:
        copy.wait_send()
    a_leave()
    b_leave()
    g_leave()
    f_arrive()
    f_leave()

    def finish_term(k, carry):
        source = lax.rem(chan + CHAN - k, CHAN)
        term_copy(source, source).wait_recv()
        target = lax.rem(chan + k, CHAN)
        term_copy(target, chan).wait_send()
        return carry

    def finish_proj(k, carry):
        source = lax.rem(me + SEQ - k, SEQ)
        proj_copy(source, source).wait_recv()
        target = lax.rem(me + k, SEQ)
        proj_copy(target, me).wait_send()
        return carry

    lax.fori_loop(1, CHAN, finish_term, 0)
    lax.fori_loop(1, SEQ, finish_proj, 0)
    own_f.wait()
    own_p.wait()
    own_t.wait()


def finish_kernel(sig_ref, token_ref, proj_ref, output_ref, token_grad_ref, proj_grad_ref, one_ref, two_ref):
    for n, ref in enumerate((output_ref, one_ref, two_ref)):
        for half in range(2):
            block = sig_ref[:, n, half * CH : (half + 1) * CH, :].reshape(INNER, INNER)
            ref[half * INNER : (half + 1) * INNER, :] = block.T
    token_grad_ref[...] = sum(token_ref[k].astype(F32) for k in range(CHAN))
    proj_grad_ref[...] = sum(proj_ref[k].astype(F32) for k in range(SEQ))


def shards(tokens, in_proj, filter_one, filter_two, out_grad):
    rows, width = tokens.shape
    depth = in_proj.shape[0]
    anywhere = pl.BlockSpec(memory_space=pl.ANY)
    dma = pltpu.SemaphoreType.DMA
    block = (SEQ, 3, 2 * CH, INNER)
    fwd, bwd, dft, idft, twiddle = tables()
    arrived = pl.pallas_call(
        chain_kernel,
        out_shape=(
            jax.ShapeDtypeStruct(block, F32),
            jax.ShapeDtypeStruct((CHAN, rows, width), BF16),
            jax.ShapeDtypeStruct((SEQ, 3, depth // SEQ, width), BF16),
        ),
        in_specs=[anywhere] * 10,
        out_specs=(anywhere,) * 3,
        scratch_shapes=[
            pltpu.VMEM((CHAN, rows, width), BF16),
            pltpu.VMEM((3, depth, width), BF16),
            pltpu.VMEM((3, rows, width), F32),
            pltpu.VMEM(fwd.shape, BF16),
            pltpu.VMEM(bwd.shape, BF16),
            pltpu.VMEM(dft.shape, BF16),
            pltpu.VMEM(idft.shape, BF16),
            pltpu.VMEM(twiddle.shape, F32),
            pltpu.VMEM((depth, rows), BF16),
            pltpu.VMEM(block, F32),
            pltpu.VMEM(block, F32),
            pltpu.VMEM(block, F32),
            pltpu.VMEM(block, F32),
            pltpu.VMEM(block, BF16),
            pltpu.VMEM(block, BF16),
            pltpu.VMEM(block, F32),
            pltpu.VMEM((CHAN, rows, width), BF16),
            pltpu.VMEM((SEQ, 3, depth // SEQ, width), BF16),
            dma((10,)),
            dma((8,)),
            dma((8,)),
        ]
        + [dma((SEQ,))] * 8
        + [dma((CHAN,)), dma((CHAN,)), dma((SEQ,)), dma((SEQ,)), dma((3,))],
        compiler_params=pltpu.CompilerParams(collective_id=0, has_side_effects=True),
        name="chain",
    )(
        tokens,
        in_proj.transpose(1, 0, 2),
        filter_one,
        filter_two,
        out_grad,
        *[jnp.asarray(t) for t in (fwd, bwd, dft, idft, twiddle)],
    )
    vmem = pl.BlockSpec(memory_space=pltpu.VMEM)
    flat = jax.ShapeDtypeStruct((rows, width), F32)
    output, token_grad, proj_grad, one, two = pl.pallas_call(
        finish_kernel,
        out_shape=(flat, flat, jax.ShapeDtypeStruct((3, depth // SEQ, width), F32), flat, flat),
        in_specs=[vmem] * 3,
        out_specs=(vmem,) * 5,
        name="finish",
    )(*arrived)
    return output, token_grad, proj_grad.transpose(1, 0, 2), one, two


def solution(mesh):
    in_specs = (
        P("seq", "chan"),
        P(None, None, "chan"),
        P("seq", "chan"),
        P("seq", "chan"),
        P("seq", "chan"),
    )
    out_specs = (
        P("seq", "chan"),
        P("seq", "chan"),
        P("seq", None, "chan"),
        P("seq", "chan"),
        P("seq", "chan"),
    )
    return jax.shard_map(shards, mesh=mesh, in_specs=in_specs, out_specs=out_specs, check_vma=False)
```

```python
import functools

import jax
import jax.numpy as jnp
import numpy as np
from jax import lax
from jax.experimental import pallas as pl
from jax.experimental.pallas import tpu as pltpu
from jax.sharding import PartitionSpec as P

OUTER = 32
INNER = 128
LENGTH = OUTER * INNER
CH = 8
ROWS = OUTER * CH
BF16 = jnp.bfloat16
F32 = jnp.float32


def split_const(matrix):
    high = matrix.astype(np.float32).astype(BF16)
    low = (matrix - high.astype(np.float64)).astype(np.float32).astype(BF16)
    return high, low


def tables():
    outer = np.arange(OUTER)
    inner = np.arange(INNER)
    shifted = outer + 0.25
    theta = 2 * np.pi * np.outer(shifted, outer) / OUTER
    eye = np.eye(CH)
    forward = np.concatenate([np.kron(np.cos(theta), eye), np.kron(-np.sin(theta), eye)], axis=0)
    backward = np.concatenate([np.kron(np.cos(theta.T), eye), np.kron(-np.sin(theta.T), eye)], axis=1) / LENGTH
    psi = 2 * np.pi * (np.outer(inner, inner) % INNER) / INNER
    cos, sin = np.cos(psi), np.sin(psi)
    dft = np.block([[cos, -sin], [sin, cos]])
    idft = np.block([[cos, sin], [-sin, cos]])
    phi = np.repeat(2 * np.pi * np.outer(shifted, inner) / LENGTH, CH, axis=0)
    fwd = np.concatenate(split_const(forward), axis=1)
    bwd = np.concatenate(split_const(backward), axis=1)
    dft2 = np.concatenate(split_const(dft), axis=0)
    idft2 = np.concatenate(split_const(idft), axis=0)
    twiddle = np.stack([np.cos(phi), np.sin(phi)]).astype(np.float32)
    return fwd, bwd, dft2, idft2, twiddle


def halves(value):
    high = value.astype(BF16)
    low = (value - high.astype(F32)).astype(BF16)
    return high, low


def product(left, right):
    return jnp.dot(left, right, preferred_element_type=F32)


def thrice(table, axis):
    high, low = jnp.split(table, 2, axis=axis)
    return jnp.concatenate([high, low, high], axis=axis)


def to_spectra(signals, fwd_ref, dft_ref, cos, sin):
    high, low = halves(jnp.concatenate(signals, axis=1))
    stage = product(thrice(fwd_ref[...], 1), jnp.concatenate([high, high, low], axis=0))
    rows = []
    for n in range(len(signals)):
        real = stage[:ROWS, n * INNER : (n + 1) * INNER]
        imag = stage[ROWS:, n * INNER : (n + 1) * INNER]
        rows.append(jnp.concatenate([real * cos + imag * sin, imag * cos - real * sin], axis=1))
    high, low = halves(jnp.concatenate(rows, axis=0))
    out = product(jnp.concatenate([high, high, low], axis=1), thrice(dft_ref[...], 0))
    return [
        (out[n * ROWS : (n + 1) * ROWS, :INNER], out[n * ROWS : (n + 1) * ROWS, INNER:])
        for n in range(len(signals))
    ]


def to_signals(spectra, bwd_ref, idft_ref, cos, sin):
    stacked = jnp.concatenate([jnp.concatenate(pair, axis=1) for pair in spectra], axis=0)
    high, low = halves(stacked)
    out = product(jnp.concatenate([high, high, low], axis=1), thrice(idft_ref[...], 0))
    columns = []
    for n in range(len(spectra)):
        real = out[n * ROWS : (n + 1) * ROWS, :INNER]
        imag = out[n * ROWS : (n + 1) * ROWS, INNER:]
        columns.append(jnp.concatenate([real * cos - imag * sin, imag * cos + real * sin], axis=0))
    high, low = halves(jnp.concatenate(columns, axis=1))
    signals = product(thrice(bwd_ref[...], 1), jnp.concatenate([high, high, low], axis=0))
    return [signals[:, n * INNER : (n + 1) * INNER] for n in range(len(spectra))]


def times(first, second):
    return first[0] * second[0] - first[1] * second[1], first[0] * second[1] + first[1] * second[0]


def times_conj(first, second):
    return first[0] * second[0] + first[1] * second[1], first[1] * second[0] - first[0] * second[1]


SEQ = 16
CHAN = 8
RING = 4
MESH = pl.DeviceIdType.MESH


def to_blocks(array):
    return [array[n * INNER : (n + 1) * INNER, :].T.reshape(SEQ, CH, INNER) for n in range(2)]


def chain_kernel(
    tok_hbm, w_hbm, one_hbm, two_hbm, grad_hbm, fwd_hbm, bwd_hbm, dft_hbm, idft_hbm, twiddle_hbm,
    sig_out, token_out, proj_out,
    tok, weights, local, fwd, bwd, dft, idft, twiddle, tok_t,
    send_a, recv_a, send_b, recv_b, send_g, recv_g, send_f, send_t,
    slabs, send_y, recv_y, send_z, recv_z, send_q,
    load_sem, tok_send, tok_recv, a_send, a_recv, b_send, b_recv, g_send, g_recv, f_send, f_recv,
    t_send, t_recv, y_send, y_recv, z_send, z_recv, q_send, q_recv, own_sem,
):
    me = lax.axis_index("seq")
    chan = lax.axis_index("chan")
    core = lax.rem(chan, 2)
    chip = lax.div(chan, 2)
    plane = lax.div(me, RING)
    row = lax.rem(me, RING)

    loads = [
        pltpu.make_async_copy(source, target, load_sem.at[n])
        for n, (source, target) in enumerate(
            [
                (tok_hbm, tok.at[chan]),
                (one_hbm, local.at[0]),
                (two_hbm, local.at[1]),
                (grad_hbm, local.at[2]),
                (w_hbm, weights),
                (fwd_hbm, fwd),
                (dft_hbm, dft),
                (twiddle_hbm, twiddle),
                (bwd_hbm, bwd),
                (idft_hbm, idft),
            ]
        )
    ]
    for load in loads:
        load.start()

    barrier = pltpu.get_barrier_semaphore()

    def greet_seq(k, carry):
        pl.semaphore_signal(
            barrier, inc=1, device_id=(lax.rem(me + k, SEQ), chan), device_id_type=MESH
        )
        return carry

    def greet_chan(k, carry):
        pl.semaphore_signal(
            barrier, inc=1, device_id=(me, lax.rem(chan + k, CHAN)), device_id_type=MESH
        )
        return carry

    lax.fori_loop(1, CHAN, greet_chan, 0)
    lax.fori_loop(1, SEQ, greet_seq, 0)
    for n in range(3):
        loads[1 + n].wait()
    for n in range(3):
        for half, block in enumerate(to_blocks(local[n])):
            send_a[:, n, half * CH : (half + 1) * CH, :] = block
    pl.semaphore_wait(barrier, SEQ + CHAN - 2)

    def token_copy(source, slot, send, target):
        return pltpu.make_async_remote_copy(
            src_ref=source,
            dst_ref=tok.at[slot],
            send_sem=tok_send.at[send],
            recv_sem=tok_recv.at[slot],
            device_id=(me, target),
            device_id_type=MESH,
        )

    def across(k):
        return lax.rem(chip + k, RING) * 2 + core

    sibling = chip * 2 + (1 - core)
    own_sends = [token_copy(tok_hbm, chan, k, across(k)) for k in (2, 1, 3)]
    own_sends.append(token_copy(tok_hbm, chan, 0, sibling))
    for copy in own_sends:
        copy.start()

    def exchange(send, recv, send_sem, recv_sem):
        def copy(target, slot):
            return pltpu.make_async_remote_copy(
                src_ref=send.at[target],
                dst_ref=recv.at[slot],
                send_sem=send_sem.at[target],
                recv_sem=recv_sem.at[slot],
                device_id=(target, chan),
                device_id_type=MESH,
            )

        def start(k, carry):
            copy(lax.rem(me + k, SEQ), me).start()
            return carry

        def wait_recv(k, carry):
            source = lax.rem(me + SEQ - k, SEQ)
            copy(source, source).wait_recv()
            return carry

        def wait_send(k, carry):
            target = lax.rem(me + k, SEQ)
            copy(target, me).wait_send()
            return carry

        return tuple(
            functools.partial(lax.fori_loop, 1, SEQ, step, 0) for step in (start, wait_recv, wait_send)
        )

    a_start, a_arrive, a_leave = exchange(send_a, recv_a, a_send, a_recv)
    b_start, b_arrive, b_leave = exchange(send_b, recv_b, b_send, b_recv)
    g_start, g_arrive, g_leave = exchange(send_g, recv_g, g_send, g_recv)
    f_start, f_arrive, f_leave = exchange(send_f, sig_out, f_send, f_recv)

    a_start()
    recv_a[me] = send_a[me]

    loads[0].wait()
    loads[4].wait()
    relays = []
    for n, k in enumerate((1, 3, 2)):
        slot = lax.rem(chip + RING - k, RING) * 2 + core
        token_copy(tok.at[slot], slot, 4 + n, sibling).wait_recv()
        relay = token_copy(tok.at[slot], slot, 4 + n, sibling)
        relay.start()
        relays.append(relay)
    for k in range(RING):
        slot = lax.rem(chip + k, RING) * 2 + (1 - core)
        token_copy(tok.at[slot], slot, 0, sibling).wait_recv()

    full = jnp.concatenate([tok[k] for k in range(CHAN)], axis=1)
    w_flat = jnp.concatenate([weights[j] for j in range(3)], axis=1)
    projected = product(full, w_flat)
    for n in range(3):
        for half, block in enumerate(to_blocks(projected[:, n * INNER : (n + 1) * INNER])):
            send_b[:, n, half * CH : (half + 1) * CH, :] = block
    b_start()
    recv_b[me] = send_b[me]

    for k in range(CHAN):
        tok_t[k * INNER : (k + 1) * INNER, :] = tok[k].T
    for n in range(5, 10):
        loads[n].wait()
    a_arrive()
    cos, sin = twiddle[0], twiddle[1]
    filter_one, filter_two, out_grad = [recv_a[:, n].reshape(ROWS, INNER) for n in range(3)]
    spec_one, spec_two = to_spectra([filter_one, filter_two], fwd, dft, cos, sin)

    b_arrive()
    values, gate_one, gate_two = [recv_b[:, n].reshape(ROWS, INNER) for n in range(3)]
    grad_two = out_grad * gate_two
    spec_values, spec_grad_two = to_spectra([values, grad_two], fwd, dft, cos, sin)
    mixed_one, grad_inner = to_signals(
        [times(spec_one, spec_values), times_conj(spec_grad_two, spec_two)], bwd, idft, cos, sin
    )
    inner = gate_one * mixed_one
    grad_one = grad_inner * gate_one
    spec_inner, spec_grad_one = to_spectra([inner, grad_one], fwd, dft, cos, sin)
    mixed_two, grad_values = to_signals(
        [times(spec_two, spec_inner), times_conj(spec_grad_one, spec_one)], bwd, idft, cos, sin
    )
    for n, grad in enumerate((grad_values, grad_inner * mixed_one, out_grad * mixed_two)):
        send_g[:, n] = grad.astype(BF16).reshape(SEQ, 2 * CH, INNER)
    g_start()
    recv_g[me] = send_g[me]
    filter_two_grad, filter_one_grad = to_signals(
        [times_conj(spec_grad_two, spec_inner), times_conj(spec_grad_one, spec_values)], bwd, idft, cos, sin
    )
    for n, signal in enumerate((gate_two * mixed_two, filter_one_grad, filter_two_grad)):
        send_f[:, n] = signal.astype(BF16).reshape(SEQ, 2 * CH, INNER)
    f_start()
    own_f = pltpu.make_async_copy(send_f.at[me], sig_out.at[me], own_sem.at[0])
    own_f.start()

    g_arrive()
    columns = []
    for n in range(3):
        arrived = recv_g[:, n].astype(F32)
        columns.append(
            jnp.concatenate(
                [
                    arrived[:, half * CH : (half + 1) * CH, :].reshape(INNER, INNER).T.astype(BF16)
                    for half in range(2)
                ],
                axis=0,
            )
        )
    grads = jnp.concatenate(columns, axis=1)

    def y_copy(step, target, slot):
        return pltpu.make_async_remote_copy(
            src_ref=send_y.at[step, target],
            dst_ref=recv_y.at[step, slot],
            send_sem=y_send.at[step * RING + target],
            recv_sem=y_recv.at[step * RING + slot],
            device_id=(plane * RING + target, chan),
            device_id_type=MESH,
        )

    def z_copy(step, target, slot):
        return pltpu.make_async_remote_copy(
            src_ref=send_z.at[step],
            dst_ref=recv_z.at[slot],
            send_sem=z_send.at[step],
            recv_sem=z_recv.at[slot],
            device_id=(target * RING + row, chan),
            device_id_type=MESH,
        )

    def q_copy(side, step, target, slot):
        return pltpu.make_async_remote_copy(
            src_ref=send_q.at[side, step],
            dst_ref=proj_out.at[side, slot],
            send_sem=q_send.at[side * RING + step],
            recv_sem=q_recv.at[side * RING + slot],
            device_id=(target, chan),
            device_id_type=MESH,
        )

    def term_copy(target, slot):
        return pltpu.make_async_remote_copy(
            src_ref=send_t.at[target],
            dst_ref=token_out.at[slot],
            send_sem=t_send.at[target],
            recv_sem=t_recv.at[slot],
            device_id=(me, target),
            device_id_type=MESH,
        )

    depth = 1024 // SEQ
    part = depth // 2
    first_sends = []
    for i, step in enumerate((2, 1, 3, 4)):
        target_plane = lax.rem(plane + step, RING)
        slab = product(
            tok_t[pl.ds(pl.multiple_of(target_plane * (RING * depth), 256), RING * depth), :], grads
        )
        slabs[i] = slab
        rounded = slab.astype(BF16)
        for n in range(RING):
            for j in range(3):
                cut = rounded[n * depth : (n + 1) * depth, j * INNER : (j + 1) * INNER]
                send_y[i, n, j] = cut[:part]
                send_z[i, n, j] = cut[part:]
        for n in (2, 1, 3):
            first_sends.append(y_copy(i, lax.rem(row + n, RING), row))
            first_sends[-1].start()
        if step < 4:
            first_sends.append(z_copy(i, target_plane, plane))
            first_sends[-1].start()
        base = lax.rem(chip + step, RING) * 2
        columns = pl.ds(pl.multiple_of(base * INNER, 256), 256)
        w_rows = jnp.concatenate([weights[j, columns, :] for j in range(3)], axis=1)
        terms = lax.dot_general(grads, w_rows, (((1,), (1,)), ((), ())), preferred_element_type=F32)
        for n in range(2):
            send_t[base + n] = terms[:, n * INNER : (n + 1) * INNER].astype(BF16)
        if step < 4:
            term_copy(base + core, chan).start()
        term_copy(base + (1 - core), chan).start()
    own_t = pltpu.make_async_copy(send_t.at[chan], token_out.at[chan], own_sem.at[2])
    own_t.start()

    rows_y = [lax.rem(row + k, RING) for k in range(RING)]
    planes_z = [lax.rem(plane + k, RING) for k in range(RING)]
    second_sends = []

    def sum_y(i):
        for source in rows_y[1:]:
            y_copy(i, source, source).wait_recv()
        mine = slabs[i, pl.ds(pl.multiple_of(row * depth, depth), part), :]
        for j in range(3):
            total = mine[:, j * INNER : (j + 1) * INNER]
            for source in rows_y[1:]:
                total += recv_y[i, source, j].astype(F32)
            send_q[0, i, j] = total.astype(BF16)

    for i, step in enumerate((2, 1, 3)):
        sum_y(i)
        second_sends.append(q_copy(0, i, planes_z[step] * RING + row, plane))
        second_sends[-1].start()
    for source in planes_z[1:]:
        z_copy(0, source, source).wait_recv()
    for n in (2, 1, 3, 0):
        target = rows_y[n]
        mine = slabs[3, pl.ds(pl.multiple_of(target * depth + part, part), part), :]
        for j in range(3):
            total = mine[:, j * INNER : (j + 1) * INNER]
            for source in planes_z[1:]:
                total += recv_z[source, target, j].astype(F32)
            send_q[1, n, j] = total.astype(BF16)
        if n > 0:
            second_sends.append(q_copy(1, n, plane * RING + target, row))
            second_sends[-1].start()
    sum_y(3)
    own_y = pltpu.make_async_copy(send_q.at[0, 3], proj_out.at[0, plane], own_sem.at[1])
    own_y.start()
    own_z = pltpu.make_async_copy(send_q.at[1, 0], proj_out.at[1, row], own_sem.at[3])
    own_z.start()

    for copy in own_sends + relays:
        copy.wait_send()
    a_leave()
    b_leave()
    g_leave()
    f_arrive()
    f_leave()

    def finish_term(k, carry):
        source = lax.rem(chan + CHAN - k, CHAN)
        term_copy(source, source).wait_recv()
        target = lax.rem(chan + k, CHAN)
        term_copy(target, chan).wait_send()
        return carry

    lax.fori_loop(1, CHAN, finish_term, 0)
    for k in range(1, RING):
        q_copy(0, 0, me, planes_z[k]).wait_recv()
        q_copy(1, 0, me, rows_y[k]).wait_recv()
    for copy in first_sends + second_sends:
        copy.wait_send()
    own_f.wait()
    own_y.wait()
    own_z.wait()
    own_t.wait()


def finish_kernel(sig_ref, token_ref, proj_ref, output_ref, token_grad_ref, proj_grad_ref, one_ref, two_ref):
    for n, ref in enumerate((output_ref, one_ref, two_ref)):
        for half in range(2):
            block = sig_ref[:, n, half * CH : (half + 1) * CH, :].astype(F32).reshape(INNER, INNER)
            ref[half * INNER : (half + 1) * INNER, :] = block.T
    token_grad_ref[...] = sum(token_ref[k].astype(F32) for k in range(CHAN))
    part = proj_ref.shape[3]
    for side in range(2):
        proj_grad_ref[:, side * part : (side + 1) * part, :] = sum(
            proj_ref[side, k].astype(F32) for k in range(RING)
        )


def shards(tokens, in_proj, filter_one, filter_two, out_grad):
    rows, width = tokens.shape
    depth = in_proj.shape[0]
    anywhere = pl.BlockSpec(memory_space=pl.ANY)
    dma = pltpu.SemaphoreType.DMA
    block = (SEQ, 3, 2 * CH, INNER)
    fwd, bwd, dft, idft, twiddle = tables()
    arrived = pl.pallas_call(
        chain_kernel,
        out_shape=(
            jax.ShapeDtypeStruct(block, BF16),
            jax.ShapeDtypeStruct((CHAN, rows, width), BF16),
            jax.ShapeDtypeStruct((2, RING, 3, depth // SEQ // 2, width), BF16),
        ),
        in_specs=[anywhere] * 10,
        out_specs=(anywhere,) * 3,
        scratch_shapes=[
            pltpu.VMEM((CHAN, rows, width), BF16),
            pltpu.VMEM((3, depth, width), BF16),
            pltpu.VMEM((3, rows, width), F32),
            pltpu.VMEM(fwd.shape, BF16),
            pltpu.VMEM(bwd.shape, BF16),
            pltpu.VMEM(dft.shape, BF16),
            pltpu.VMEM(idft.shape, BF16),
            pltpu.VMEM(twiddle.shape, F32),
            pltpu.VMEM((depth, rows), BF16),
            pltpu.VMEM(block, F32),
            pltpu.VMEM(block, F32),
            pltpu.VMEM(block, F32),
            pltpu.VMEM(block, F32),
            pltpu.VMEM(block, BF16),
            pltpu.VMEM(block, BF16),
            pltpu.VMEM(block, BF16),
            pltpu.VMEM((CHAN, rows, width), BF16),
            pltpu.VMEM((RING, depth // RING, 3 * width), F32),
            pltpu.VMEM((RING, RING, 3, depth // SEQ // 2, width), BF16),
            pltpu.VMEM((RING, RING, 3, depth // SEQ // 2, width), BF16),
            pltpu.VMEM((RING, RING, 3, depth // SEQ // 2, width), BF16),
            pltpu.VMEM((RING, RING, 3, depth // SEQ // 2, width), BF16),
            pltpu.VMEM((2, RING, 3, depth // SEQ // 2, width), BF16),
            dma((10,)),
            dma((8,)),
            dma((8,)),
        ]
        + [dma((SEQ,))] * 8
        + [dma((CHAN,))] * 2
        + [dma((SEQ,))] * 2
        + [dma((RING,))] * 2
        + [dma((2 * RING,))] * 2
        + [dma((4,))],
        compiler_params=pltpu.CompilerParams(collective_id=0, has_side_effects=True),
        name="chain",
    )(
        tokens,
        in_proj.transpose(1, 0, 2),
        filter_one,
        filter_two,
        out_grad,
        *[jnp.asarray(t) for t in (fwd, bwd, dft, idft, twiddle)],
    )
    vmem = pl.BlockSpec(memory_space=pltpu.VMEM)
    flat = jax.ShapeDtypeStruct((rows, width), F32)
    output, token_grad, proj_grad, one, two = pl.pallas_call(
        finish_kernel,
        out_shape=(flat, flat, jax.ShapeDtypeStruct((3, depth // SEQ, width), F32), flat, flat),
        in_specs=[vmem] * 3,
        out_specs=(vmem,) * 5,
        name="finish",
    )(*arrived)
    return output, token_grad, proj_grad.transpose(1, 0, 2), one, two


def solution(mesh):
    in_specs = (
        P("seq", "chan"),
        P(None, None, "chan"),
        P("seq", "chan"),
        P("seq", "chan"),
        P("seq", "chan"),
    )
    out_specs = (
        P("seq", "chan"),
        P("seq", "chan"),
        P("seq", None, "chan"),
        P("seq", "chan"),
        P("seq", "chan"),
    )
    return jax.shard_map(shards, mesh=mesh, in_specs=in_specs, out_specs=out_specs, check_vma=False)
```

```python
import functools

import jax
import jax.numpy as jnp
import numpy as np
from jax import lax
from jax.experimental import pallas as pl
from jax.experimental.pallas import tpu as pltpu
from jax.sharding import PartitionSpec as P

OUTER = 32
INNER = 128
LENGTH = OUTER * INNER
CH = 8
ROWS = OUTER * CH
BF16 = jnp.bfloat16
F32 = jnp.float32


def split_const(matrix):
    high = matrix.astype(np.float32).astype(BF16)
    low = (matrix - high.astype(np.float64)).astype(np.float32).astype(BF16)
    return high, low


def tables():
    outer = np.arange(OUTER)
    inner = np.arange(INNER)
    shifted = outer + 0.25
    theta = 2 * np.pi * np.outer(shifted, outer) / OUTER
    eye = np.eye(CH)
    forward = np.concatenate([np.kron(np.cos(theta), eye), np.kron(-np.sin(theta), eye)], axis=0)
    backward = np.concatenate([np.kron(np.cos(theta.T), eye), np.kron(-np.sin(theta.T), eye)], axis=1) / LENGTH
    psi = 2 * np.pi * (np.outer(inner, inner) % INNER) / INNER
    cos, sin = np.cos(psi), np.sin(psi)
    dft = np.block([[cos, -sin], [sin, cos]])
    idft = np.block([[cos, sin], [-sin, cos]])
    phi = np.repeat(2 * np.pi * np.outer(shifted, inner) / LENGTH, CH, axis=0)
    fwd = np.concatenate(split_const(forward), axis=1)
    bwd = np.concatenate(split_const(backward), axis=1)
    dft2 = np.concatenate(split_const(dft), axis=0)
    idft2 = np.concatenate(split_const(idft), axis=0)
    twiddle = np.stack([np.cos(phi), np.sin(phi)]).astype(np.float32)
    return fwd, bwd, dft2, idft2, twiddle


def halves(value):
    high = value.astype(BF16)
    low = (value - high.astype(F32)).astype(BF16)
    return high, low


def product(left, right):
    return jnp.dot(left, right, preferred_element_type=F32)


def thrice(table, axis):
    high, low = jnp.split(table, 2, axis=axis)
    return jnp.concatenate([high, low, high], axis=axis)


def to_spectra(signals, fwd_ref, dft_ref, cos, sin):
    high, low = halves(jnp.concatenate(signals, axis=1))
    stage = product(thrice(fwd_ref[...], 1), jnp.concatenate([high, high, low], axis=0))
    rows = []
    for n in range(len(signals)):
        real = stage[:ROWS, n * INNER : (n + 1) * INNER]
        imag = stage[ROWS:, n * INNER : (n + 1) * INNER]
        rows.append(jnp.concatenate([real * cos + imag * sin, imag * cos - real * sin], axis=1))
    high, low = halves(jnp.concatenate(rows, axis=0))
    out = product(jnp.concatenate([high, high, low], axis=1), thrice(dft_ref[...], 0))
    return [
        (out[n * ROWS : (n + 1) * ROWS, :INNER], out[n * ROWS : (n + 1) * ROWS, INNER:])
        for n in range(len(signals))
    ]


def to_signals(spectra, bwd_ref, idft_ref, cos, sin):
    stacked = jnp.concatenate([jnp.concatenate(pair, axis=1) for pair in spectra], axis=0)
    high, low = halves(stacked)
    out = product(jnp.concatenate([high, high, low], axis=1), thrice(idft_ref[...], 0))
    columns = []
    for n in range(len(spectra)):
        real = out[n * ROWS : (n + 1) * ROWS, :INNER]
        imag = out[n * ROWS : (n + 1) * ROWS, INNER:]
        columns.append(jnp.concatenate([real * cos - imag * sin, imag * cos + real * sin], axis=0))
    high, low = halves(jnp.concatenate(columns, axis=1))
    signals = product(thrice(bwd_ref[...], 1), jnp.concatenate([high, high, low], axis=0))
    return [signals[:, n * INNER : (n + 1) * INNER] for n in range(len(spectra))]


def times(first, second):
    return first[0] * second[0] - first[1] * second[1], first[0] * second[1] + first[1] * second[0]


def times_conj(first, second):
    return first[0] * second[0] + first[1] * second[1], first[1] * second[0] - first[0] * second[1]


SEQ = 16
CHAN = 8
RING = 4
GRAD_ORDER = (1, 0, 2)
GRAD_GROUPS = ((0, 1), (1, 2))
MESH = pl.DeviceIdType.MESH


def to_blocks(array):
    return [array[n * INNER : (n + 1) * INNER, :].T.reshape(SEQ, CH, INNER) for n in range(2)]


def chain_kernel(
    tok_hbm, w_hbm, one_hbm, two_hbm, grad_hbm, fwd_hbm, bwd_hbm, dft_hbm, idft_hbm, twiddle_hbm,
    sig_out, token_out, proj_out,
    tok, weights, local, fwd, bwd, dft, idft, twiddle, tok_t,
    send_a, recv_a, send_b, recv_b, send_c, recv_c, send_g, recv_g, send_h, recv_h, send_f, send_t,
    slabs, send_y, recv_y, send_z, recv_z, send_q,
    load_sem, tok_send, tok_recv, a_send, a_recv, b_send, b_recv, c_send, c_recv, g_send, g_recv,
    h_send, h_recv, f_send, f_recv,
    t_send, t_recv, y_send, y_recv, z_send, z_recv, q_send, q_recv, own_sem,
):
    me = lax.axis_index("seq")
    chan = lax.axis_index("chan")
    core = lax.rem(chan, 2)
    chip = lax.div(chan, 2)
    plane = lax.div(me, RING)
    row = lax.rem(me, RING)

    loads = [
        pltpu.make_async_copy(source, target, load_sem.at[n])
        for n, (source, target) in enumerate(
            [
                (tok_hbm, tok.at[chan]),
                (one_hbm, local.at[0]),
                (two_hbm, local.at[1]),
                (grad_hbm, local.at[2]),
                (w_hbm, weights),
                (fwd_hbm, fwd),
                (dft_hbm, dft),
                (twiddle_hbm, twiddle),
                (bwd_hbm, bwd),
                (idft_hbm, idft),
            ]
        )
    ]
    for load in loads:
        load.start()

    barrier = pltpu.get_barrier_semaphore()

    def greet_seq(k, carry):
        pl.semaphore_signal(
            barrier, inc=1, device_id=(lax.rem(me + k, SEQ), chan), device_id_type=MESH
        )
        return carry

    def greet_chan(k, carry):
        pl.semaphore_signal(
            barrier, inc=1, device_id=(me, lax.rem(chan + k, CHAN)), device_id_type=MESH
        )
        return carry

    lax.fori_loop(1, CHAN, greet_chan, 0)
    lax.fori_loop(1, SEQ, greet_seq, 0)
    for n in range(3):
        loads[1 + n].wait()
    for n in range(3):
        for half, block in enumerate(to_blocks(local[n])):
            send_a[:, n, half * CH : (half + 1) * CH, :] = block
    pl.semaphore_wait(barrier, SEQ + CHAN - 2)

    def token_copy(source, slot, send, target):
        return pltpu.make_async_remote_copy(
            src_ref=source,
            dst_ref=tok.at[slot],
            send_sem=tok_send.at[send],
            recv_sem=tok_recv.at[slot],
            device_id=(me, target),
            device_id_type=MESH,
        )

    def across(k):
        return lax.rem(chip + k, RING) * 2 + core

    sibling = chip * 2 + (1 - core)
    own_sends = [token_copy(tok_hbm, chan, k, across(k)) for k in (2, 1, 3)]
    own_sends.append(token_copy(tok_hbm, chan, 0, sibling))
    for copy in own_sends:
        copy.start()

    def exchange(send, recv, send_sem, recv_sem):
        def copy(target, slot):
            return pltpu.make_async_remote_copy(
                src_ref=send.at[target],
                dst_ref=recv.at[slot],
                send_sem=send_sem.at[target],
                recv_sem=recv_sem.at[slot],
                device_id=(target, chan),
                device_id_type=MESH,
            )

        def start(k, carry):
            copy(lax.rem(me + k, SEQ), me).start()
            return carry

        def wait_recv(k, carry):
            source = lax.rem(me + SEQ - k, SEQ)
            copy(source, source).wait_recv()
            return carry

        def wait_send(k, carry):
            target = lax.rem(me + k, SEQ)
            copy(target, me).wait_send()
            return carry

        return tuple(
            functools.partial(lax.fori_loop, 1, SEQ, step, 0) for step in (start, wait_recv, wait_send)
        )

    a_start, a_arrive, a_leave = exchange(send_a, recv_a, a_send, a_recv)
    b_start, b_arrive, b_leave = exchange(send_b, recv_b, b_send, b_recv)
    c_start, c_arrive, c_leave = exchange(send_c, recv_c, c_send, c_recv)
    g_start, g_arrive, g_leave = exchange(send_g, recv_g, g_send, g_recv)
    h_start, h_arrive, h_leave = exchange(send_h, recv_h, h_send, h_recv)
    f_start, f_arrive, f_leave = exchange(send_f, sig_out, f_send, f_recv)

    a_start()
    recv_a[me] = send_a[me]

    loads[0].wait()
    loads[4].wait()
    relays = []
    for n, k in enumerate((1, 3, 2)):
        slot = lax.rem(chip + RING - k, RING) * 2 + core
        token_copy(tok.at[slot], slot, 4 + n, sibling).wait_recv()
        relay = token_copy(tok.at[slot], slot, 4 + n, sibling)
        relay.start()
        relays.append(relay)
    for k in range(RING):
        slot = lax.rem(chip + k, RING) * 2 + (1 - core)
        token_copy(tok.at[slot], slot, 0, sibling).wait_recv()

    full = jnp.concatenate([tok[k] for k in range(CHAN)], axis=1)
    projected = product(full, jnp.concatenate([weights[0], weights[2]], axis=1))
    for n in range(2):
        for half, block in enumerate(to_blocks(projected[:, n * INNER : (n + 1) * INNER])):
            send_b[:, n, half * CH : (half + 1) * CH, :] = block
    b_start()
    for half, block in enumerate(to_blocks(product(full, weights[1]))):
        send_c[:, 0, half * CH : (half + 1) * CH, :] = block
    c_start()
    recv_b[me] = send_b[me]
    recv_c[me] = send_c[me]

    for k in range(CHAN):
        tok_t[k * INNER : (k + 1) * INNER, :] = tok[k].T
    for n in range(5, 10):
        loads[n].wait()
    a_arrive()
    cos, sin = twiddle[0], twiddle[1]
    filter_one, filter_two, out_grad = [recv_a[:, n].reshape(ROWS, INNER) for n in range(3)]
    spec_one, spec_two = to_spectra([filter_one, filter_two], fwd, dft, cos, sin)

    b_arrive()
    values, gate_two = [recv_b[:, n].reshape(ROWS, INNER) for n in range(2)]
    grad_two = out_grad * gate_two
    spec_values, spec_grad_two = to_spectra([values, grad_two], fwd, dft, cos, sin)
    mixed_one, grad_inner = to_signals(
        [times(spec_one, spec_values), times_conj(spec_grad_two, spec_two)], bwd, idft, cos, sin
    )
    c_arrive()
    gate_one = recv_c[:, 0].reshape(ROWS, INNER)
    send_g[:, 0] = (grad_inner * mixed_one).astype(BF16).reshape(SEQ, 2 * CH, INNER)
    g_start()
    recv_g[me] = send_g[me]
    inner = gate_one * mixed_one
    grad_one = grad_inner * gate_one
    spec_inner, spec_grad_one = to_spectra([inner, grad_one], fwd, dft, cos, sin)
    mixed_two, grad_values = to_signals(
        [times(spec_two, spec_inner), times_conj(spec_grad_one, spec_one)], bwd, idft, cos, sin
    )
    for n, grad in enumerate((grad_values, out_grad * mixed_two)):
        send_h[:, n] = grad.astype(BF16).reshape(SEQ, 2 * CH, INNER)
    h_start()
    recv_h[me] = send_h[me]

    depth = 1024 // SEQ
    part = depth // 2

    def y_copy(group, step, target, slot):
        cut = pl.ds(*GRAD_GROUPS[group])
        base = (group * RING + step) * RING
        return pltpu.make_async_remote_copy(
            src_ref=send_y.at[step, target, cut],
            dst_ref=recv_y.at[step, slot, cut],
            send_sem=y_send.at[base + target],
            recv_sem=y_recv.at[base + slot],
            device_id=(plane * RING + target, chan),
            device_id_type=MESH,
        )

    def z_copy(group, step, target, slot):
        cut = pl.ds(*GRAD_GROUPS[group])
        return pltpu.make_async_remote_copy(
            src_ref=send_z.at[step, cut],
            dst_ref=recv_z.at[slot, cut],
            send_sem=z_send.at[group * RING + step],
            recv_sem=z_recv.at[group * RING + slot],
            device_id=(target * RING + row, chan),
            device_id_type=MESH,
        )

    def q_copy(side, step, target, slot):
        return pltpu.make_async_remote_copy(
            src_ref=send_q.at[side, step],
            dst_ref=proj_out.at[side, slot],
            send_sem=q_send.at[side * RING + step],
            recv_sem=q_recv.at[side * RING + slot],
            device_id=(target, chan),
            device_id_type=MESH,
        )

    def term_copy(target, slot):
        return pltpu.make_async_remote_copy(
            src_ref=send_t.at[target],
            dst_ref=token_out.at[slot],
            send_sem=t_send.at[target],
            recv_sem=t_recv.at[slot],
            device_id=(me, target),
            device_id_type=MESH,
        )

    def by_token(arrived):
        arrived = arrived.astype(F32)
        return jnp.concatenate(
            [
                arrived[:, half * CH : (half + 1) * CH, :].reshape(INNER, INNER).T.astype(BF16)
                for half in range(2)
            ],
            axis=0,
        )

    first_sends = []

    def proj_step(group, i, grads):
        step = (2, 1, 3, 4)[i]
        target_plane = lax.rem(plane + step, RING)
        slab = product(
            tok_t[pl.ds(pl.multiple_of(target_plane * (RING * depth), 256), RING * depth), :], grads
        )
        first, count = GRAD_GROUPS[group]
        slabs[i, :, first * INNER : (first + count) * INNER] = slab
        rounded = slab.astype(BF16)
        for n in range(RING):
            for j in range(count):
                cut = rounded[n * depth : (n + 1) * depth, j * INNER : (j + 1) * INNER]
                send_y[i, n, first + j] = cut[:part]
                send_z[i, first + j, n] = cut[part:]
        for n in (2, 1, 3):
            first_sends.append(y_copy(group, i, lax.rem(row + n, RING), row))
            first_sends[-1].start()
        if step < 4:
            first_sends.append(z_copy(group, i, target_plane, plane))
            first_sends[-1].start()

    g_arrive()
    early = by_token(recv_g[:, 0])
    for i in range(RING):
        proj_step(0, i, early)

    filter_two_grad, filter_one_grad = to_signals(
        [times_conj(spec_grad_two, spec_inner), times_conj(spec_grad_one, spec_values)], bwd, idft, cos, sin
    )
    for n, signal in enumerate((gate_two * mixed_two, filter_one_grad, filter_two_grad)):
        send_f[:, n] = signal.astype(BF16).reshape(SEQ, 2 * CH, INNER)
    f_start()
    own_f = pltpu.make_async_copy(send_f.at[me], sig_out.at[me], own_sem.at[0])
    own_f.start()

    h_arrive()
    late = jnp.concatenate([by_token(recv_h[:, n]) for n in range(2)], axis=1)
    grads = jnp.concatenate([early, late], axis=1)

    for i, step in enumerate((2, 1, 3, 4)):
        proj_step(1, i, late)
        base = lax.rem(chip + step, RING) * 2
        columns = pl.ds(pl.multiple_of(base * INNER, 256), 256)
        w_rows = jnp.concatenate([weights[j, columns, :] for j in GRAD_ORDER], axis=1)
        terms = lax.dot_general(grads, w_rows, (((1,), (1,)), ((), ())), preferred_element_type=F32)
        for n in range(2):
            send_t[base + n] = terms[:, n * INNER : (n + 1) * INNER].astype(BF16)
        if step < 4:
            term_copy(base + core, chan).start()
        term_copy(base + (1 - core), chan).start()
    own_t = pltpu.make_async_copy(send_t.at[chan], token_out.at[chan], own_sem.at[2])
    own_t.start()

    rows_y = [lax.rem(row + k, RING) for k in range(RING)]
    planes_z = [lax.rem(plane + k, RING) for k in range(RING)]
    second_sends = []

    def sum_y(i):
        for source in rows_y[1:]:
            y_copy(0, i, source, source).wait_recv()
            y_copy(1, i, source, source).wait_recv()
        mine = slabs[i, pl.ds(pl.multiple_of(row * depth, depth), part), :]
        for j in range(3):
            total = mine[:, j * INNER : (j + 1) * INNER]
            for source in rows_y[1:]:
                total += recv_y[i, source, j].astype(F32)
            send_q[0, i, j] = total.astype(BF16)

    for i, step in enumerate((2, 1, 3)):
        sum_y(i)
        second_sends.append(q_copy(0, i, planes_z[step] * RING + row, plane))
        second_sends[-1].start()
    for source in planes_z[1:]:
        z_copy(0, 0, source, source).wait_recv()
        z_copy(1, 0, source, source).wait_recv()
    for n in (2, 1, 3, 0):
        target = rows_y[n]
        mine = slabs[3, pl.ds(pl.multiple_of(target * depth + part, part), part), :]
        for j in range(3):
            total = mine[:, j * INNER : (j + 1) * INNER]
            for source in planes_z[1:]:
                total += recv_z[source, j, target].astype(F32)
            send_q[1, n, j] = total.astype(BF16)
        if n > 0:
            second_sends.append(q_copy(1, n, plane * RING + target, row))
            second_sends[-1].start()
    sum_y(3)
    own_y = pltpu.make_async_copy(send_q.at[0, 3], proj_out.at[0, plane], own_sem.at[1])
    own_y.start()
    own_z = pltpu.make_async_copy(send_q.at[1, 0], proj_out.at[1, row], own_sem.at[3])
    own_z.start()

    for copy in own_sends + relays:
        copy.wait_send()
    a_leave()
    b_leave()
    c_leave()
    g_leave()
    h_leave()
    f_arrive()
    f_leave()

    def finish_term(k, carry):
        source = lax.rem(chan + CHAN - k, CHAN)
        term_copy(source, source).wait_recv()
        target = lax.rem(chan + k, CHAN)
        term_copy(target, chan).wait_send()
        return carry

    lax.fori_loop(1, CHAN, finish_term, 0)
    for k in range(1, RING):
        q_copy(0, 0, me, planes_z[k]).wait_recv()
        q_copy(1, 0, me, rows_y[k]).wait_recv()
    for copy in first_sends + second_sends:
        copy.wait_send()
    own_f.wait()
    own_y.wait()
    own_z.wait()
    own_t.wait()


def finish_kernel(sig_ref, token_ref, proj_ref, output_ref, token_grad_ref, proj_grad_ref, one_ref, two_ref):
    for n, ref in enumerate((output_ref, one_ref, two_ref)):
        for half in range(2):
            block = sig_ref[:, n, half * CH : (half + 1) * CH, :].astype(F32).reshape(INNER, INNER)
            ref[half * INNER : (half + 1) * INNER, :] = block.T
    token_grad_ref[...] = sum(token_ref[k].astype(F32) for k in range(CHAN))
    part = proj_ref.shape[3]
    for side in range(2):
        for n, j in enumerate(GRAD_ORDER):
            proj_grad_ref[j, side * part : (side + 1) * part, :] = sum(
                proj_ref[side, k, n].astype(F32) for k in range(RING)
            )


def shards(tokens, in_proj, filter_one, filter_two, out_grad):
    rows, width = tokens.shape
    depth = in_proj.shape[0]
    anywhere = pl.BlockSpec(memory_space=pl.ANY)
    dma = pltpu.SemaphoreType.DMA
    block, two, one = [(SEQ, n, 2 * CH, INNER) for n in (3, 2, 1)]
    fwd, bwd, dft, idft, twiddle = tables()
    arrived = pl.pallas_call(
        chain_kernel,
        out_shape=(
            jax.ShapeDtypeStruct(block, BF16),
            jax.ShapeDtypeStruct((CHAN, rows, width), BF16),
            jax.ShapeDtypeStruct((2, RING, 3, depth // SEQ // 2, width), BF16),
        ),
        in_specs=[anywhere] * 10,
        out_specs=(anywhere,) * 3,
        scratch_shapes=[
            pltpu.VMEM((CHAN, rows, width), BF16),
            pltpu.VMEM((3, depth, width), BF16),
            pltpu.VMEM((3, rows, width), F32),
            pltpu.VMEM(fwd.shape, BF16),
            pltpu.VMEM(bwd.shape, BF16),
            pltpu.VMEM(dft.shape, BF16),
            pltpu.VMEM(idft.shape, BF16),
            pltpu.VMEM(twiddle.shape, F32),
            pltpu.VMEM((depth, rows), BF16),
            pltpu.VMEM(block, F32),
            pltpu.VMEM(block, F32),
            pltpu.VMEM(two, F32),
            pltpu.VMEM(two, F32),
            pltpu.VMEM(one, F32),
            pltpu.VMEM(one, F32),
            pltpu.VMEM(one, BF16),
            pltpu.VMEM(one, BF16),
            pltpu.VMEM(two, BF16),
            pltpu.VMEM(two, BF16),
            pltpu.VMEM(block, BF16),
            pltpu.VMEM((CHAN, rows, width), BF16),
            pltpu.VMEM((RING, depth // RING, 3 * width), F32),
            pltpu.VMEM((RING, RING, 3, depth // SEQ // 2, width), BF16),
            pltpu.VMEM((RING, RING, 3, depth // SEQ // 2, width), BF16),
            pltpu.VMEM((RING, 3, RING, depth // SEQ // 2, width), BF16),
            pltpu.VMEM((RING, 3, RING, depth // SEQ // 2, width), BF16),
            pltpu.VMEM((2, RING, 3, depth // SEQ // 2, width), BF16),
            dma((10,)),
            dma((8,)),
            dma((8,)),
        ]
        + [dma((SEQ,))] * 12
        + [dma((CHAN,))] * 2
        + [dma((2 * SEQ,))] * 2
        + [dma((2 * RING,))] * 2
        + [dma((2 * RING,))] * 2
        + [dma((4,))],
        compiler_params=pltpu.CompilerParams(collective_id=0, has_side_effects=True),
        name="chain",
    )(
        tokens,
        in_proj.transpose(1, 0, 2),
        filter_one,
        filter_two,
        out_grad,
        *[jnp.asarray(t) for t in (fwd, bwd, dft, idft, twiddle)],
    )
    vmem = pl.BlockSpec(memory_space=pltpu.VMEM)
    flat = jax.ShapeDtypeStruct((rows, width), F32)
    output, token_grad, proj_grad, one, two = pl.pallas_call(
        finish_kernel,
        out_shape=(flat, flat, jax.ShapeDtypeStruct((3, depth // SEQ, width), F32), flat, flat),
        in_specs=[vmem] * 3,
        out_specs=(vmem,) * 5,
        name="finish",
    )(*arrived)
    return output, token_grad, proj_grad.transpose(1, 0, 2), one, two


def solution(mesh):
    in_specs = (
        P("seq", "chan"),
        P(None, None, "chan"),
        P("seq", "chan"),
        P("seq", "chan"),
        P("seq", "chan"),
    )
    out_specs = (
        P("seq", "chan"),
        P("seq", "chan"),
        P("seq", None, "chan"),
        P("seq", "chan"),
        P("seq", "chan"),
    )
    return jax.shard_map(shards, mesh=mesh, in_specs=in_specs, out_specs=out_specs, check_vma=False)
```

```python
import functools

import jax
import jax.numpy as jnp
import numpy as np
from jax import lax
from jax.experimental import pallas as pl
from jax.experimental.pallas import tpu as pltpu
from jax.sharding import PartitionSpec as P

OUTER = 32
INNER = 128
LENGTH = OUTER * INNER
CH = 8
ROWS = OUTER * CH
BF16 = jnp.bfloat16
F32 = jnp.float32


def split_const(matrix):
    high = matrix.astype(np.float32).astype(BF16)
    low = (matrix - high.astype(np.float64)).astype(np.float32).astype(BF16)
    return high, low


def tables():
    outer = np.arange(OUTER)
    inner = np.arange(INNER)
    shifted = outer + 0.25
    theta = 2 * np.pi * np.outer(shifted, outer) / OUTER
    eye = np.eye(CH)
    forward = np.concatenate([np.kron(np.cos(theta), eye), np.kron(-np.sin(theta), eye)], axis=0)
    backward = np.concatenate([np.kron(np.cos(theta.T), eye), np.kron(-np.sin(theta.T), eye)], axis=1) / LENGTH
    psi = 2 * np.pi * (np.outer(inner, inner) % INNER) / INNER
    cos, sin = np.cos(psi), np.sin(psi)
    dft = np.block([[cos, -sin], [sin, cos]])
    idft = np.block([[cos, sin], [-sin, cos]])
    phi = np.repeat(2 * np.pi * np.outer(shifted, inner) / LENGTH, CH, axis=0)
    fwd = np.concatenate(split_const(forward), axis=1)
    bwd = np.concatenate(split_const(backward), axis=1)
    dft2 = np.concatenate(split_const(dft), axis=0)
    idft2 = np.concatenate(split_const(idft), axis=0)
    twiddle = np.stack([np.cos(phi), np.sin(phi)]).astype(np.float32)
    return fwd, bwd, dft2, idft2, twiddle


def halves(value):
    high = value.astype(BF16)
    low = (value - high.astype(F32)).astype(BF16)
    return high, low


def product(left, right):
    return jnp.dot(left, right, preferred_element_type=F32)


def thrice(table, axis):
    high, low = jnp.split(table, 2, axis=axis)
    return jnp.concatenate([high, low, high], axis=axis)


def to_spectra(signals, fwd_ref, dft_ref, cos, sin):
    high, low = halves(jnp.concatenate(signals, axis=1))
    stage = product(thrice(fwd_ref[...], 1), jnp.concatenate([high, high, low], axis=0))
    rows = []
    for n in range(len(signals)):
        real = stage[:ROWS, n * INNER : (n + 1) * INNER]
        imag = stage[ROWS:, n * INNER : (n + 1) * INNER]
        rows.append(jnp.concatenate([real * cos + imag * sin, imag * cos - real * sin], axis=1))
    high, low = halves(jnp.concatenate(rows, axis=0))
    out = product(jnp.concatenate([high, high, low], axis=1), thrice(dft_ref[...], 0))
    return [
        (out[n * ROWS : (n + 1) * ROWS, :INNER], out[n * ROWS : (n + 1) * ROWS, INNER:])
        for n in range(len(signals))
    ]


def to_signals(spectra, bwd_ref, idft_ref, cos, sin):
    stacked = jnp.concatenate([jnp.concatenate(pair, axis=1) for pair in spectra], axis=0)
    high, low = halves(stacked)
    out = product(jnp.concatenate([high, high, low], axis=1), thrice(idft_ref[...], 0))
    columns = []
    for n in range(len(spectra)):
        real = out[n * ROWS : (n + 1) * ROWS, :INNER]
        imag = out[n * ROWS : (n + 1) * ROWS, INNER:]
        columns.append(jnp.concatenate([real * cos - imag * sin, imag * cos + real * sin], axis=0))
    high, low = halves(jnp.concatenate(columns, axis=1))
    signals = product(thrice(bwd_ref[...], 1), jnp.concatenate([high, high, low], axis=0))
    return [signals[:, n * INNER : (n + 1) * INNER] for n in range(len(spectra))]


def times(first, second):
    return first[0] * second[0] - first[1] * second[1], first[0] * second[1] + first[1] * second[0]


def times_conj(first, second):
    return first[0] * second[0] + first[1] * second[1], first[1] * second[0] - first[0] * second[1]


SEQ = 16
CHAN = 8
RING = 4
GRAD_ORDER = (1, 0, 2)
GRAD_GROUPS = ((0, 1), (1, 2))
MESH = pl.DeviceIdType.MESH


def to_blocks(array):
    return [array[n * INNER : (n + 1) * INNER, :].T.reshape(SEQ, CH, INNER) for n in range(2)]


def chain_kernel(
    tok_hbm, w_hbm, one_hbm, two_hbm, grad_hbm, fwd_hbm, bwd_hbm, dft_hbm, idft_hbm, twiddle_hbm,
    sig_out, token_out, proj_out,
    tok, weights, local, fwd, bwd, dft, idft, twiddle, tok_t,
    send_a, recv_a, send_b, recv_b, send_c, recv_c, send_g, recv_g, send_h, recv_h, send_f, send_t,
    slabs, send_y, recv_y, send_z, recv_z, send_q,
    load_sem, tok_send, tok_recv, a_send, a_recv, b_send, b_recv, c_send, c_recv, g_send, g_recv,
    h_send, h_recv, f_send, f_recv,
    t_send, t_recv, y_send, y_recv, z_send, z_recv, q_send, q_recv, own_sem, ready,
):
    me = lax.axis_index("seq")
    chan = lax.axis_index("chan")
    core = lax.rem(chan, 2)
    chip = lax.div(chan, 2)
    plane = lax.div(me, RING)
    row = lax.rem(me, RING)

    loads = [
        pltpu.make_async_copy(source, target, load_sem.at[n])
        for n, (source, target) in enumerate(
            [
                (tok_hbm, tok.at[chan]),
                (one_hbm, local.at[0]),
                (two_hbm, local.at[1]),
                (grad_hbm, local.at[2]),
                (w_hbm, weights),
                (fwd_hbm, fwd),
                (dft_hbm, dft),
                (twiddle_hbm, twiddle),
                (bwd_hbm, bwd),
                (idft_hbm, idft),
            ]
        )
    ]
    for load in loads:
        load.start()

    barrier = pltpu.get_barrier_semaphore()

    beside_y = [(plane * RING + lax.rem(row + k, RING), chan) for k in range(1, RING)]
    beside_z = [(lax.rem(plane + k, RING) * RING + row, chan) for k in range(1, RING)]

    def greet_chan(k, carry):
        pl.semaphore_signal(
            barrier, inc=1, device_id=(me, lax.rem(chan + k, CHAN)), device_id_type=MESH
        )
        return carry

    lax.fori_loop(1, CHAN, greet_chan, 0)
    for target in beside_z + beside_y:
        pl.semaphore_signal(barrier, inc=1, device_id=target, device_id_type=MESH)
    for n in range(3):
        loads[1 + n].wait()
    for n in range(3):
        for half, block in enumerate(to_blocks(local[n])):
            send_a[:, n, half * CH : (half + 1) * CH, :] = block
    pl.semaphore_wait(barrier, CHAN - 1 + 2 * (RING - 1))

    def token_copy(source, slot, send, target):
        return pltpu.make_async_remote_copy(
            src_ref=source,
            dst_ref=tok.at[slot],
            send_sem=tok_send.at[send],
            recv_sem=tok_recv.at[slot],
            device_id=(me, target),
            device_id_type=MESH,
        )

    def across(k):
        return lax.rem(chip + k, RING) * 2 + core

    sibling = chip * 2 + (1 - core)
    own_sends = [token_copy(tok_hbm, chan, k, across(k)) for k in (2, 1, 3)]
    own_sends.append(token_copy(tok_hbm, chan, 0, sibling))
    for copy in own_sends:
        copy.start()
    for target in beside_y:
        pl.semaphore_signal(ready, inc=1, device_id=target, device_id_type=MESH)

    def exchange(send, recv, send_sem, recv_sem):
        def copy(target, slot):
            return pltpu.make_async_remote_copy(
                src_ref=send.at[target],
                dst_ref=recv.at[slot],
                send_sem=send_sem.at[target],
                recv_sem=recv_sem.at[slot],
                device_id=(target, chan),
                device_id_type=MESH,
            )

        def start(k, carry):
            copy(lax.rem(me + k, SEQ), me).start()
            return carry

        def wait_recv(k, carry):
            source = lax.rem(me + SEQ - k, SEQ)
            copy(source, source).wait_recv()
            return carry

        def wait_send(k, carry):
            target = lax.rem(me + k, SEQ)
            copy(target, me).wait_send()
            return carry

        return tuple(
            functools.partial(lax.fori_loop, 1, SEQ, step, 0) for step in (start, wait_recv, wait_send)
        )

    a_start, a_arrive, a_leave = exchange(send_a, recv_a, a_send, a_recv)
    b_start, b_arrive, b_leave = exchange(send_b, recv_b, b_send, b_recv)
    c_start, c_arrive, c_leave = exchange(send_c, recv_c, c_send, c_recv)
    g_start, g_arrive, g_leave = exchange(send_g, recv_g, g_send, g_recv)
    h_start, h_arrive, h_leave = exchange(send_h, recv_h, h_send, h_recv)
    f_start, f_arrive, f_leave = exchange(send_f, sig_out, f_send, f_recv)

    pl.semaphore_wait(ready, RING - 1)
    a_start()
    recv_a[me] = send_a[me]

    loads[0].wait()
    loads[4].wait()
    relays = []
    for n, k in enumerate((1, 3, 2)):
        slot = lax.rem(chip + RING - k, RING) * 2 + core
        token_copy(tok.at[slot], slot, 4 + n, sibling).wait_recv()
        relay = token_copy(tok.at[slot], slot, 4 + n, sibling)
        relay.start()
        relays.append(relay)
    for k in range(RING):
        slot = lax.rem(chip + k, RING) * 2 + (1 - core)
        token_copy(tok.at[slot], slot, 0, sibling).wait_recv()

    full = jnp.concatenate([tok[k] for k in range(CHAN)], axis=1)
    projected = product(full, jnp.concatenate([weights[0], weights[2]], axis=1))
    for n in range(2):
        for half, block in enumerate(to_blocks(projected[:, n * INNER : (n + 1) * INNER])):
            send_b[:, n, half * CH : (half + 1) * CH, :] = block
    b_start()
    for half, block in enumerate(to_blocks(product(full, weights[1]))):
        send_c[:, 0, half * CH : (half + 1) * CH, :] = block
    c_start()
    recv_b[me] = send_b[me]
    recv_c[me] = send_c[me]

    for k in range(CHAN):
        tok_t[k * INNER : (k + 1) * INNER, :] = tok[k].T
    for n in range(5, 10):
        loads[n].wait()
    a_arrive()
    cos, sin = twiddle[0], twiddle[1]
    filter_one, filter_two, out_grad = [recv_a[:, n].reshape(ROWS, INNER) for n in range(3)]
    spec_one, spec_two = to_spectra([filter_one, filter_two], fwd, dft, cos, sin)

    b_arrive()
    values, gate_two = [recv_b[:, n].reshape(ROWS, INNER) for n in range(2)]
    grad_two = out_grad * gate_two
    spec_values, spec_grad_two = to_spectra([values, grad_two], fwd, dft, cos, sin)
    mixed_one, grad_inner = to_signals(
        [times(spec_one, spec_values), times_conj(spec_grad_two, spec_two)], bwd, idft, cos, sin
    )
    c_arrive()
    gate_one = recv_c[:, 0].reshape(ROWS, INNER)
    send_g[:, 0] = (grad_inner * mixed_one).astype(BF16).reshape(SEQ, 2 * CH, INNER)
    g_start()
    recv_g[me] = send_g[me]
    inner = gate_one * mixed_one
    grad_one = grad_inner * gate_one
    spec_inner, spec_grad_one = to_spectra([inner, grad_one], fwd, dft, cos, sin)
    mixed_two, grad_values = to_signals(
        [times(spec_two, spec_inner), times_conj(spec_grad_one, spec_one)], bwd, idft, cos, sin
    )
    for n, grad in enumerate((grad_values, out_grad * mixed_two)):
        send_h[:, n] = grad.astype(BF16).reshape(SEQ, 2 * CH, INNER)
    h_start()
    recv_h[me] = send_h[me]

    depth = 1024 // SEQ
    part = depth // 2

    def y_copy(group, step, target, slot):
        cut = pl.ds(*GRAD_GROUPS[group])
        base = (group * RING + step) * RING
        return pltpu.make_async_remote_copy(
            src_ref=send_y.at[step, target, cut],
            dst_ref=recv_y.at[step, slot, cut],
            send_sem=y_send.at[base + target],
            recv_sem=y_recv.at[base + slot],
            device_id=(plane * RING + target, chan),
            device_id_type=MESH,
        )

    def z_copy(group, step, target, slot):
        cut = pl.ds(*GRAD_GROUPS[group])
        return pltpu.make_async_remote_copy(
            src_ref=send_z.at[step, cut],
            dst_ref=recv_z.at[slot, cut],
            send_sem=z_send.at[group * RING + step],
            recv_sem=z_recv.at[group * RING + slot],
            device_id=(target * RING + row, chan),
            device_id_type=MESH,
        )

    def q_copy(side, step, target, slot):
        return pltpu.make_async_remote_copy(
            src_ref=send_q.at[side, step],
            dst_ref=proj_out.at[side, slot],
            send_sem=q_send.at[side * RING + step],
            recv_sem=q_recv.at[side * RING + slot],
            device_id=(target, chan),
            device_id_type=MESH,
        )

    def term_copy(target, slot):
        return pltpu.make_async_remote_copy(
            src_ref=send_t.at[target],
            dst_ref=token_out.at[slot],
            send_sem=t_send.at[target],
            recv_sem=t_recv.at[slot],
            device_id=(me, target),
            device_id_type=MESH,
        )

    def by_token(arrived):
        arrived = arrived.astype(F32)
        return jnp.concatenate(
            [
                arrived[:, half * CH : (half + 1) * CH, :].reshape(INNER, INNER).T.astype(BF16)
                for half in range(2)
            ],
            axis=0,
        )

    first_sends = []

    def proj_step(group, i, grads):
        step = (2, 1, 3, 4)[i]
        target_plane = lax.rem(plane + step, RING)
        slab = product(
            tok_t[pl.ds(pl.multiple_of(target_plane * (RING * depth), 256), RING * depth), :], grads
        )
        first, count = GRAD_GROUPS[group]
        slabs[i, :, first * INNER : (first + count) * INNER] = slab
        rounded = slab.astype(BF16)
        for n in range(RING):
            for j in range(count):
                cut = rounded[n * depth : (n + 1) * depth, j * INNER : (j + 1) * INNER]
                send_y[i, n, first + j] = cut[:part]
                send_z[i, first + j, n] = cut[part:]
        for n in (2, 1, 3):
            first_sends.append(y_copy(group, i, lax.rem(row + n, RING), row))
            first_sends[-1].start()
        if step < 4:
            first_sends.append(z_copy(group, i, target_plane, plane))
            first_sends[-1].start()

    g_arrive()
    early = by_token(recv_g[:, 0])
    for i in range(RING):
        proj_step(0, i, early)

    filter_two_grad, filter_one_grad = to_signals(
        [times_conj(spec_grad_two, spec_inner), times_conj(spec_grad_one, spec_values)], bwd, idft, cos, sin
    )
    for n, signal in enumerate((gate_two * mixed_two, filter_one_grad, filter_two_grad)):
        send_f[:, n] = signal.astype(BF16).reshape(SEQ, 2 * CH, INNER)
    f_start()
    own_f = pltpu.make_async_copy(send_f.at[me], sig_out.at[me], own_sem.at[0])
    own_f.start()

    h_arrive()
    late = jnp.concatenate([by_token(recv_h[:, n]) for n in range(2)], axis=1)
    grads = jnp.concatenate([early, late], axis=1)

    for i, step in enumerate((2, 1, 3, 4)):
        proj_step(1, i, late)
        base = lax.rem(chip + step, RING) * 2
        columns = pl.ds(pl.multiple_of(base * INNER, 256), 256)
        w_rows = jnp.concatenate([weights[j, columns, :] for j in GRAD_ORDER], axis=1)
        terms = lax.dot_general(grads, w_rows, (((1,), (1,)), ((), ())), preferred_element_type=F32)
        for n in range(2):
            send_t[base + n] = terms[:, n * INNER : (n + 1) * INNER].astype(BF16)
        if step < 4:
            term_copy(base + core, chan).start()
        term_copy(base + (1 - core), chan).start()
    own_t = pltpu.make_async_copy(send_t.at[chan], token_out.at[chan], own_sem.at[2])
    own_t.start()

    rows_y = [lax.rem(row + k, RING) for k in range(RING)]
    planes_z = [lax.rem(plane + k, RING) for k in range(RING)]
    second_sends = []

    def sum_y(i):
        for source in rows_y[1:]:
            y_copy(0, i, source, source).wait_recv()
            y_copy(1, i, source, source).wait_recv()
        mine = slabs[i, pl.ds(pl.multiple_of(row * depth, depth), part), :]
        for j in range(3):
            total = mine[:, j * INNER : (j + 1) * INNER]
            for source in rows_y[1:]:
                total += recv_y[i, source, j].astype(F32)
            send_q[0, i, j] = total.astype(BF16)

    for i, step in enumerate((2, 1, 3)):
        sum_y(i)
        second_sends.append(q_copy(0, i, planes_z[step] * RING + row, plane))
        second_sends[-1].start()
    for source in planes_z[1:]:
        z_copy(0, 0, source, source).wait_recv()
        z_copy(1, 0, source, source).wait_recv()
    for n in (2, 1, 3, 0):
        target = rows_y[n]
        mine = slabs[3, pl.ds(pl.multiple_of(target * depth + part, part), part), :]
        for j in range(3):
            total = mine[:, j * INNER : (j + 1) * INNER]
            for source in planes_z[1:]:
                total += recv_z[source, j, target].astype(F32)
            send_q[1, n, j] = total.astype(BF16)
        if n > 0:
            second_sends.append(q_copy(1, n, plane * RING + target, row))
            second_sends[-1].start()
    sum_y(3)
    own_y = pltpu.make_async_copy(send_q.at[0, 3], proj_out.at[0, plane], own_sem.at[1])
    own_y.start()
    own_z = pltpu.make_async_copy(send_q.at[1, 0], proj_out.at[1, row], own_sem.at[3])
    own_z.start()

    for copy in own_sends + relays:
        copy.wait_send()
    a_leave()
    b_leave()
    c_leave()
    g_leave()
    h_leave()
    f_arrive()
    f_leave()

    def finish_term(k, carry):
        source = lax.rem(chan + CHAN - k, CHAN)
        term_copy(source, source).wait_recv()
        target = lax.rem(chan + k, CHAN)
        term_copy(target, chan).wait_send()
        return carry

    lax.fori_loop(1, CHAN, finish_term, 0)
    for k in range(1, RING):
        q_copy(0, 0, me, planes_z[k]).wait_recv()
        q_copy(1, 0, me, rows_y[k]).wait_recv()
    for copy in first_sends + second_sends:
        copy.wait_send()
    own_f.wait()
    own_y.wait()
    own_z.wait()
    own_t.wait()


def finish_kernel(sig_ref, token_ref, proj_ref, output_ref, token_grad_ref, proj_grad_ref, one_ref, two_ref):
    for n, ref in enumerate((output_ref, one_ref, two_ref)):
        for half in range(2):
            block = sig_ref[:, n, half * CH : (half + 1) * CH, :].astype(F32).reshape(INNER, INNER)
            ref[half * INNER : (half + 1) * INNER, :] = block.T
    token_grad_ref[...] = sum(token_ref[k].astype(F32) for k in range(CHAN))
    part = proj_ref.shape[3]
    for side in range(2):
        for n, j in enumerate(GRAD_ORDER):
            proj_grad_ref[j, side * part : (side + 1) * part, :] = sum(
                proj_ref[side, k, n].astype(F32) for k in range(RING)
            )


def shards(tokens, in_proj, filter_one, filter_two, out_grad):
    rows, width = tokens.shape
    depth = in_proj.shape[0]
    anywhere = pl.BlockSpec(memory_space=pl.ANY)
    dma = pltpu.SemaphoreType.DMA
    block, two, one = [(SEQ, n, 2 * CH, INNER) for n in (3, 2, 1)]
    fwd, bwd, dft, idft, twiddle = tables()
    arrived = pl.pallas_call(
        chain_kernel,
        out_shape=(
            jax.ShapeDtypeStruct(block, BF16),
            jax.ShapeDtypeStruct((CHAN, rows, width), BF16),
            jax.ShapeDtypeStruct((2, RING, 3, depth // SEQ // 2, width), BF16),
        ),
        in_specs=[anywhere] * 10,
        out_specs=(anywhere,) * 3,
        scratch_shapes=[
            pltpu.VMEM((CHAN, rows, width), BF16),
            pltpu.VMEM((3, depth, width), BF16),
            pltpu.VMEM((3, rows, width), F32),
            pltpu.VMEM(fwd.shape, BF16),
            pltpu.VMEM(bwd.shape, BF16),
            pltpu.VMEM(dft.shape, BF16),
            pltpu.VMEM(idft.shape, BF16),
            pltpu.VMEM(twiddle.shape, F32),
            pltpu.VMEM((depth, rows), BF16),
            pltpu.VMEM(block, F32),
            pltpu.VMEM(block, F32),
            pltpu.VMEM(two, F32),
            pltpu.VMEM(two, F32),
            pltpu.VMEM(one, F32),
            pltpu.VMEM(one, F32),
            pltpu.VMEM(one, BF16),
            pltpu.VMEM(one, BF16),
            pltpu.VMEM(two, BF16),
            pltpu.VMEM(two, BF16),
            pltpu.VMEM(block, BF16),
            pltpu.VMEM((CHAN, rows, width), BF16),
            pltpu.VMEM((RING, depth // RING, 3 * width), F32),
            pltpu.VMEM((RING, RING, 3, depth // SEQ // 2, width), BF16),
            pltpu.VMEM((RING, RING, 3, depth // SEQ // 2, width), BF16),
            pltpu.VMEM((RING, 3, RING, depth // SEQ // 2, width), BF16),
            pltpu.VMEM((RING, 3, RING, depth // SEQ // 2, width), BF16),
            pltpu.VMEM((2, RING, 3, depth // SEQ // 2, width), BF16),
            dma((10,)),
            dma((8,)),
            dma((8,)),
        ]
        + [dma((SEQ,))] * 12
        + [dma((CHAN,))] * 2
        + [dma((2 * SEQ,))] * 2
        + [dma((2 * RING,))] * 2
        + [dma((2 * RING,))] * 2
        + [dma((4,)), pltpu.SemaphoreType.REGULAR],
        compiler_params=pltpu.CompilerParams(collective_id=0, has_side_effects=True),
        name="chain",
    )(
        tokens,
        in_proj.transpose(1, 0, 2),
        filter_one,
        filter_two,
        out_grad,
        *[jnp.asarray(t) for t in (fwd, bwd, dft, idft, twiddle)],
    )
    vmem = pl.BlockSpec(memory_space=pltpu.VMEM)
    flat = jax.ShapeDtypeStruct((rows, width), F32)
    output, token_grad, proj_grad, one, two = pl.pallas_call(
        finish_kernel,
        out_shape=(flat, flat, jax.ShapeDtypeStruct((3, depth // SEQ, width), F32), flat, flat),
        in_specs=[vmem] * 3,
        out_specs=(vmem,) * 5,
        name="finish",
    )(*arrived)
    return output, token_grad, proj_grad.transpose(1, 0, 2), one, two


def solution(mesh):
    in_specs = (
        P("seq", "chan"),
        P(None, None, "chan"),
        P("seq", "chan"),
        P("seq", "chan"),
        P("seq", "chan"),
    )
    out_specs = (
        P("seq", "chan"),
        P("seq", "chan"),
        P("seq", None, "chan"),
        P("seq", "chan"),
        P("seq", "chan"),
    )
    return jax.shard_map(shards, mesh=mesh, in_specs=in_specs, out_specs=out_specs, check_vma=False)
```

```python
import functools

import jax
import jax.numpy as jnp
import numpy as np
from jax import lax
from jax.experimental import pallas as pl
from jax.experimental.pallas import tpu as pltpu
from jax.sharding import PartitionSpec as P

OUTER = 32
INNER = 128
LENGTH = OUTER * INNER
CH = 8
ROWS = OUTER * CH
BF16 = jnp.bfloat16
F32 = jnp.float32


def split_const(matrix):
    high = matrix.astype(np.float32).astype(BF16)
    low = (matrix - high.astype(np.float64)).astype(np.float32).astype(BF16)
    return high, low


def tables():
    outer = np.arange(OUTER)
    inner = np.arange(INNER)
    shifted = outer + 0.25
    theta = 2 * np.pi * np.outer(shifted, outer) / OUTER
    eye = np.eye(CH)
    forward = np.concatenate([np.kron(np.cos(theta), eye), np.kron(-np.sin(theta), eye)], axis=0)
    backward = np.concatenate([np.kron(np.cos(theta.T), eye), np.kron(-np.sin(theta.T), eye)], axis=1) / LENGTH
    psi = 2 * np.pi * (np.outer(inner, inner) % INNER) / INNER
    cos, sin = np.cos(psi), np.sin(psi)
    dft = np.block([[cos, -sin], [sin, cos]])
    idft = np.block([[cos, sin], [-sin, cos]])
    phi = np.repeat(2 * np.pi * np.outer(shifted, inner) / LENGTH, CH, axis=0)
    fwd = np.concatenate(split_const(forward), axis=1)
    bwd = np.concatenate(split_const(backward), axis=1)
    dft2 = np.concatenate(split_const(dft), axis=0)
    idft2 = np.concatenate(split_const(idft), axis=0)
    twiddle = np.stack([np.cos(phi), np.sin(phi)]).astype(np.float32)
    return fwd, bwd, dft2, idft2, twiddle


def halves(value):
    high = value.astype(BF16)
    low = (value - high.astype(F32)).astype(BF16)
    return high, low


def product(left, right):
    return jnp.dot(left, right, preferred_element_type=F32)


def thrice(table, axis):
    high, low = jnp.split(table, 2, axis=axis)
    return jnp.concatenate([high, low, high], axis=axis)


def to_spectra(signals, fwd_ref, dft_ref, cos, sin):
    high, low = halves(jnp.concatenate(signals, axis=1))
    stage = product(thrice(fwd_ref[...], 1), jnp.concatenate([high, high, low], axis=0))
    rows = []
    for n in range(len(signals)):
        real = stage[:ROWS, n * INNER : (n + 1) * INNER]
        imag = stage[ROWS:, n * INNER : (n + 1) * INNER]
        rows.append(jnp.concatenate([real * cos + imag * sin, imag * cos - real * sin], axis=1))
    high, low = halves(jnp.concatenate(rows, axis=0))
    out = product(jnp.concatenate([high, high, low], axis=1), thrice(dft_ref[...], 0))
    return [
        (out[n * ROWS : (n + 1) * ROWS, :INNER], out[n * ROWS : (n + 1) * ROWS, INNER:])
        for n in range(len(signals))
    ]


def to_signals(spectra, bwd_ref, idft_ref, cos, sin):
    stacked = jnp.concatenate([jnp.concatenate(pair, axis=1) for pair in spectra], axis=0)
    high, low = halves(stacked)
    out = product(jnp.concatenate([high, high, low], axis=1), thrice(idft_ref[...], 0))
    columns = []
    for n in range(len(spectra)):
        real = out[n * ROWS : (n + 1) * ROWS, :INNER]
        imag = out[n * ROWS : (n + 1) * ROWS, INNER:]
        columns.append(jnp.concatenate([real * cos - imag * sin, imag * cos + real * sin], axis=0))
    high, low = halves(jnp.concatenate(columns, axis=1))
    signals = product(thrice(bwd_ref[...], 1), jnp.concatenate([high, high, low], axis=0))
    return [signals[:, n * INNER : (n + 1) * INNER] for n in range(len(spectra))]


def times(first, second):
    return first[0] * second[0] - first[1] * second[1], first[0] * second[1] + first[1] * second[0]


def times_conj(first, second):
    return first[0] * second[0] + first[1] * second[1], first[1] * second[0] - first[0] * second[1]


SEQ = 16
CHAN = 8
RING = 4
GRAD_ORDER = (1, 0, 2)
GRAD_GROUPS = ((0, 1), (1, 2))
MESH = pl.DeviceIdType.MESH


def to_blocks(array):
    return [array[n * INNER : (n + 1) * INNER, :].T.reshape(SEQ, CH, INNER) for n in range(2)]


def chain_kernel(
    tok_hbm, w_hbm, one_hbm, two_hbm, grad_hbm, fwd_hbm, bwd_hbm, dft_hbm, idft_hbm, twiddle_hbm,
    sig_out, token_out, proj_out,
    tok, weights, local, fwd, bwd, dft, idft, twiddle, tok_t,
    send_a, recv_a, send_b, recv_b, send_c, recv_c, send_g, recv_g, send_h, recv_h, send_f, send_t,
    slabs, send_y, recv_y, send_z, recv_z, send_q,
    load_sem, tok_send, tok_recv, a_send, a_recv, b_send, b_recv, c_send, c_recv, g_send, g_recv,
    h_send, h_recv, f_send, f_recv,
    t_send, t_recv, y_send, y_recv, z_send, z_recv, q_send, q_recv, own_sem, ready,
):
    me = lax.axis_index("seq")
    chan = lax.axis_index("chan")
    core = lax.rem(chan, 2)
    chip = lax.div(chan, 2)
    plane = lax.div(me, RING)
    row = lax.rem(me, RING)

    loads = [
        pltpu.make_async_copy(source, target, load_sem.at[n])
        for n, (source, target) in enumerate(
            [
                (tok_hbm, tok.at[chan]),
                (one_hbm, local.at[0]),
                (two_hbm, local.at[1]),
                (grad_hbm, local.at[2]),
                (w_hbm, weights),
                (fwd_hbm, fwd),
                (dft_hbm, dft),
                (twiddle_hbm, twiddle),
                (bwd_hbm, bwd),
                (idft_hbm, idft),
            ]
        )
    ]
    for load in loads:
        load.start()

    barrier = pltpu.get_barrier_semaphore()

    beside_y = [(plane * RING + lax.rem(row + k, RING), chan) for k in range(1, RING)]
    beside_z = [(lax.rem(plane + k, RING) * RING + row, chan) for k in range(1, RING)]

    beside_x = [(me, lax.rem(chip + k, RING) * 2 + core) for k in range(1, RING)]
    beside_x.append((me, chip * 2 + (1 - core)))
    for target in beside_x + beside_z + beside_y:
        pl.semaphore_signal(barrier, inc=1, device_id=target, device_id_type=MESH)
    for n in range(3):
        loads[1 + n].wait()
    for n in range(3):
        for half, block in enumerate(to_blocks(local[n])):
            send_a[:, n, half * CH : (half + 1) * CH, :] = block
    pl.semaphore_wait(barrier, 1 + 3 * (RING - 1))

    def token_copy(source, slot, send, target):
        return pltpu.make_async_remote_copy(
            src_ref=source,
            dst_ref=tok.at[slot],
            send_sem=tok_send.at[send],
            recv_sem=tok_recv.at[slot],
            device_id=(me, target),
            device_id_type=MESH,
        )

    def across(k):
        return lax.rem(chip + k, RING) * 2 + core

    sibling = chip * 2 + (1 - core)
    own_sends = [token_copy(tok_hbm, chan, k, across(k)) for k in (2, 1, 3)]
    own_sends.append(token_copy(tok_hbm, chan, 0, sibling))
    for copy in own_sends:
        copy.start()
    for target in beside_y:
        pl.semaphore_signal(ready, inc=1, device_id=target, device_id_type=MESH)

    def exchange(send, recv, send_sem, recv_sem):
        def copy(target, slot):
            return pltpu.make_async_remote_copy(
                src_ref=send.at[target],
                dst_ref=recv.at[slot],
                send_sem=send_sem.at[target],
                recv_sem=recv_sem.at[slot],
                device_id=(target, chan),
                device_id_type=MESH,
            )

        def start(k, carry):
            copy(lax.rem(me + k, SEQ), me).start()
            return carry

        def wait_recv(k, carry):
            source = lax.rem(me + SEQ - k, SEQ)
            copy(source, source).wait_recv()
            return carry

        def wait_send(k, carry):
            target = lax.rem(me + k, SEQ)
            copy(target, me).wait_send()
            return carry

        return tuple(
            functools.partial(lax.fori_loop, 1, SEQ, step, 0) for step in (start, wait_recv, wait_send)
        )

    a_start, a_arrive, a_leave = exchange(send_a, recv_a, a_send, a_recv)
    b_start, b_arrive, b_leave = exchange(send_b, recv_b, b_send, b_recv)
    c_start, c_arrive, c_leave = exchange(send_c, recv_c, c_send, c_recv)
    g_start, g_arrive, g_leave = exchange(send_g, recv_g, g_send, g_recv)
    h_start, h_arrive, h_leave = exchange(send_h, recv_h, h_send, h_recv)
    f_start, f_arrive, f_leave = exchange(send_f, sig_out, f_send, f_recv)

    pl.semaphore_wait(ready, RING - 1)
    a_start()
    recv_a[me] = send_a[me]

    loads[0].wait()
    loads[4].wait()
    relays = []
    for n, k in enumerate((1, 3, 2)):
        slot = lax.rem(chip + RING - k, RING) * 2 + core
        token_copy(tok.at[slot], slot, 4 + n, sibling).wait_recv()
        relay = token_copy(tok.at[slot], slot, 4 + n, sibling)
        relay.start()
        relays.append(relay)
    for k in range(RING):
        slot = lax.rem(chip + k, RING) * 2 + (1 - core)
        token_copy(tok.at[slot], slot, 0, sibling).wait_recv()

    full = jnp.concatenate([tok[k] for k in range(CHAN)], axis=1)
    projected = product(full, jnp.concatenate([weights[0], weights[2]], axis=1))
    for n in range(2):
        for half, block in enumerate(to_blocks(projected[:, n * INNER : (n + 1) * INNER])):
            send_b[:, n, half * CH : (half + 1) * CH, :] = block
    b_start()
    for half, block in enumerate(to_blocks(product(full, weights[1]))):
        send_c[:, 0, half * CH : (half + 1) * CH, :] = block
    c_start()
    recv_b[me] = send_b[me]
    recv_c[me] = send_c[me]

    for k in range(CHAN):
        tok_t[k * INNER : (k + 1) * INNER, :] = tok[k].T
    for n in range(5, 10):
        loads[n].wait()
    a_arrive()
    cos, sin = twiddle[0], twiddle[1]
    filter_one, filter_two, out_grad = [recv_a[:, n].reshape(ROWS, INNER) for n in range(3)]
    spec_one, spec_two = to_spectra([filter_one, filter_two], fwd, dft, cos, sin)

    b_arrive()
    values, gate_two = [recv_b[:, n].reshape(ROWS, INNER) for n in range(2)]
    grad_two = out_grad * gate_two
    spec_values, spec_grad_two = to_spectra([values, grad_two], fwd, dft, cos, sin)
    mixed_one, grad_inner = to_signals(
        [times(spec_one, spec_values), times_conj(spec_grad_two, spec_two)], bwd, idft, cos, sin
    )
    c_arrive()
    gate_one = recv_c[:, 0].reshape(ROWS, INNER)
    send_g[:, 0] = (grad_inner * mixed_one).astype(BF16).reshape(SEQ, 2 * CH, INNER)
    g_start()
    recv_g[me] = send_g[me]
    inner = gate_one * mixed_one
    grad_one = grad_inner * gate_one
    spec_inner, spec_grad_one = to_spectra([inner, grad_one], fwd, dft, cos, sin)
    mixed_two, grad_values = to_signals(
        [times(spec_two, spec_inner), times_conj(spec_grad_one, spec_one)], bwd, idft, cos, sin
    )
    for n, grad in enumerate((grad_values, out_grad * mixed_two)):
        send_h[:, n] = grad.astype(BF16).reshape(SEQ, 2 * CH, INNER)
    h_start()
    recv_h[me] = send_h[me]

    depth = 1024 // SEQ
    part = depth // 2

    def y_copy(group, step, target, slot):
        cut = pl.ds(*GRAD_GROUPS[group])
        base = (group * RING + step) * RING
        return pltpu.make_async_remote_copy(
            src_ref=send_y.at[step, target, cut],
            dst_ref=recv_y.at[step, slot, cut],
            send_sem=y_send.at[base + target],
            recv_sem=y_recv.at[base + slot],
            device_id=(plane * RING + target, chan),
            device_id_type=MESH,
        )

    def z_copy(group, step, target, slot):
        cut = pl.ds(*GRAD_GROUPS[group])
        return pltpu.make_async_remote_copy(
            src_ref=send_z.at[step, cut],
            dst_ref=recv_z.at[slot, cut],
            send_sem=z_send.at[group * RING + step],
            recv_sem=z_recv.at[group * RING + slot],
            device_id=(target * RING + row, chan),
            device_id_type=MESH,
        )

    def q_copy(side, step, target, slot):
        return pltpu.make_async_remote_copy(
            src_ref=send_q.at[side, step],
            dst_ref=proj_out.at[side, slot],
            send_sem=q_send.at[side * RING + step],
            recv_sem=q_recv.at[side * RING + slot],
            device_id=(target, chan),
            device_id_type=MESH,
        )

    def term_copy(target, slot):
        return pltpu.make_async_remote_copy(
            src_ref=send_t.at[target],
            dst_ref=token_out.at[slot],
            send_sem=t_send.at[target],
            recv_sem=t_recv.at[slot],
            device_id=(me, target),
            device_id_type=MESH,
        )

    def by_token(arrived):
        arrived = arrived.astype(F32)
        return jnp.concatenate(
            [
                arrived[:, half * CH : (half + 1) * CH, :].reshape(INNER, INNER).T.astype(BF16)
                for half in range(2)
            ],
            axis=0,
        )

    first_sends = []

    def proj_step(group, i, grads):
        step = (2, 1, 3, 4)[i]
        target_plane = lax.rem(plane + step, RING)
        slab = product(
            tok_t[pl.ds(pl.multiple_of(target_plane * (RING * depth), 256), RING * depth), :], grads
        )
        first, count = GRAD_GROUPS[group]
        slabs[i, :, first * INNER : (first + count) * INNER] = slab
        rounded = slab.astype(BF16)
        for n in range(RING):
            for j in range(count):
                cut = rounded[n * depth : (n + 1) * depth, j * INNER : (j + 1) * INNER]
                send_y[i, n, first + j] = cut[:part]
                send_z[i, first + j, n] = cut[part:]
        for n in (2, 1, 3):
            first_sends.append(y_copy(group, i, lax.rem(row + n, RING), row))
            first_sends[-1].start()
        if step < 4:
            first_sends.append(z_copy(group, i, target_plane, plane))
            first_sends[-1].start()

    g_arrive()
    early = by_token(recv_g[:, 0])
    for i in range(RING):
        proj_step(0, i, early)

    filter_two_grad, filter_one_grad = to_signals(
        [times_conj(spec_grad_two, spec_inner), times_conj(spec_grad_one, spec_values)], bwd, idft, cos, sin
    )
    for n, signal in enumerate((gate_two * mixed_two, filter_one_grad, filter_two_grad)):
        send_f[:, n] = signal.astype(BF16).reshape(SEQ, 2 * CH, INNER)
    f_start()
    own_f = pltpu.make_async_copy(send_f.at[me], sig_out.at[me], own_sem.at[0])
    own_f.start()

    h_arrive()
    late = jnp.concatenate([by_token(recv_h[:, n]) for n in range(2)], axis=1)
    grads = jnp.concatenate([early, late], axis=1)

    for i, step in enumerate((2, 1, 3, 4)):
        proj_step(1, i, late)
        base = lax.rem(chip + step, RING) * 2
        columns = pl.ds(pl.multiple_of(base * INNER, 256), 256)
        w_rows = jnp.concatenate([weights[j, columns, :] for j in GRAD_ORDER], axis=1)
        terms = lax.dot_general(grads, w_rows, (((1,), (1,)), ((), ())), preferred_element_type=F32)
        for n in range(2):
            send_t[base + n] = terms[:, n * INNER : (n + 1) * INNER].astype(BF16)
        if step < 4:
            term_copy(base + core, chan).start()
        term_copy(base + (1 - core), chan).start()
    own_t = pltpu.make_async_copy(send_t.at[chan], token_out.at[chan], own_sem.at[2])
    own_t.start()

    rows_y = [lax.rem(row + k, RING) for k in range(RING)]
    planes_z = [lax.rem(plane + k, RING) for k in range(RING)]
    second_sends = []

    def sum_y(i):
        for source in rows_y[1:]:
            y_copy(0, i, source, source).wait_recv()
            y_copy(1, i, source, source).wait_recv()
        mine = slabs[i, pl.ds(pl.multiple_of(row * depth, depth), part), :]
        for j in range(3):
            total = mine[:, j * INNER : (j + 1) * INNER]
            for source in rows_y[1:]:
                total += recv_y[i, source, j].astype(F32)
            send_q[0, i, j] = total.astype(BF16)

    for i, step in enumerate((2, 1, 3)):
        sum_y(i)
        second_sends.append(q_copy(0, i, planes_z[step] * RING + row, plane))
        second_sends[-1].start()
    for source in planes_z[1:]:
        z_copy(0, 0, source, source).wait_recv()
        z_copy(1, 0, source, source).wait_recv()
    for n in (2, 1, 3, 0):
        target = rows_y[n]
        mine = slabs[3, pl.ds(pl.multiple_of(target * depth + part, part), part), :]
        for j in range(3):
            total = mine[:, j * INNER : (j + 1) * INNER]
            for source in planes_z[1:]:
                total += recv_z[source, j, target].astype(F32)
            send_q[1, n, j] = total.astype(BF16)
        if n > 0:
            second_sends.append(q_copy(1, n, plane * RING + target, row))
            second_sends[-1].start()
    sum_y(3)
    own_y = pltpu.make_async_copy(send_q.at[0, 3], proj_out.at[0, plane], own_sem.at[1])
    own_y.start()
    own_z = pltpu.make_async_copy(send_q.at[1, 0], proj_out.at[1, row], own_sem.at[3])
    own_z.start()

    for copy in own_sends + relays:
        copy.wait_send()
    a_leave()
    b_leave()
    c_leave()
    g_leave()
    h_leave()
    f_arrive()
    f_leave()

    def finish_term(k, carry):
        source = lax.rem(chan + CHAN - k, CHAN)
        term_copy(source, source).wait_recv()
        target = lax.rem(chan + k, CHAN)
        term_copy(target, chan).wait_send()
        return carry

    lax.fori_loop(1, CHAN, finish_term, 0)
    for k in range(1, RING):
        q_copy(0, 0, me, planes_z[k]).wait_recv()
        q_copy(1, 0, me, rows_y[k]).wait_recv()
    for copy in first_sends + second_sends:
        copy.wait_send()
    own_f.wait()
    own_y.wait()
    own_z.wait()
    own_t.wait()


def finish_kernel(sig_ref, token_ref, proj_ref, output_ref, token_grad_ref, proj_grad_ref, one_ref, two_ref):
    for n, ref in enumerate((output_ref, one_ref, two_ref)):
        for half in range(2):
            block = sig_ref[:, n, half * CH : (half + 1) * CH, :].astype(F32).reshape(INNER, INNER)
            ref[half * INNER : (half + 1) * INNER, :] = block.T
    token_grad_ref[...] = sum(token_ref[k].astype(F32) for k in range(CHAN))
    part = proj_ref.shape[3]
    for side in range(2):
        for n, j in enumerate(GRAD_ORDER):
            proj_grad_ref[j, side * part : (side + 1) * part, :] = sum(
                proj_ref[side, k, n].astype(F32) for k in range(RING)
            )


def shards(tokens, in_proj, filter_one, filter_two, out_grad):
    rows, width = tokens.shape
    depth = in_proj.shape[0]
    anywhere = pl.BlockSpec(memory_space=pl.ANY)
    dma = pltpu.SemaphoreType.DMA
    block, two, one = [(SEQ, n, 2 * CH, INNER) for n in (3, 2, 1)]
    fwd, bwd, dft, idft, twiddle = tables()
    arrived = pl.pallas_call(
        chain_kernel,
        out_shape=(
            jax.ShapeDtypeStruct(block, BF16),
            jax.ShapeDtypeStruct((CHAN, rows, width), BF16),
            jax.ShapeDtypeStruct((2, RING, 3, depth // SEQ // 2, width), BF16),
        ),
        in_specs=[anywhere] * 10,
        out_specs=(anywhere,) * 3,
        scratch_shapes=[
            pltpu.VMEM((CHAN, rows, width), BF16),
            pltpu.VMEM((3, depth, width), BF16),
            pltpu.VMEM((3, rows, width), F32),
            pltpu.VMEM(fwd.shape, BF16),
            pltpu.VMEM(bwd.shape, BF16),
            pltpu.VMEM(dft.shape, BF16),
            pltpu.VMEM(idft.shape, BF16),
            pltpu.VMEM(twiddle.shape, F32),
            pltpu.VMEM((depth, rows), BF16),
            pltpu.VMEM(block, F32),
            pltpu.VMEM(block, F32),
            pltpu.VMEM(two, F32),
            pltpu.VMEM(two, F32),
            pltpu.VMEM(one, F32),
            pltpu.VMEM(one, F32),
            pltpu.VMEM(one, BF16),
            pltpu.VMEM(one, BF16),
            pltpu.VMEM(two, BF16),
            pltpu.VMEM(two, BF16),
            pltpu.VMEM(block, BF16),
            pltpu.VMEM((CHAN, rows, width), BF16),
            pltpu.VMEM((RING, depth // RING, 3 * width), F32),
            pltpu.VMEM((RING, RING, 3, depth // SEQ // 2, width), BF16),
            pltpu.VMEM((RING, RING, 3, depth // SEQ // 2, width), BF16),
            pltpu.VMEM((RING, 3, RING, depth // SEQ // 2, width), BF16),
            pltpu.VMEM((RING, 3, RING, depth // SEQ // 2, width), BF16),
            pltpu.VMEM((2, RING, 3, depth // SEQ // 2, width), BF16),
            dma((10,)),
            dma((8,)),
            dma((8,)),
        ]
        + [dma((SEQ,))] * 12
        + [dma((CHAN,))] * 2
        + [dma((2 * SEQ,))] * 2
        + [dma((2 * RING,))] * 2
        + [dma((2 * RING,))] * 2
        + [dma((4,)), pltpu.SemaphoreType.REGULAR],
        compiler_params=pltpu.CompilerParams(collective_id=0, has_side_effects=True),
        name="chain",
    )(
        tokens,
        in_proj.transpose(1, 0, 2),
        filter_one,
        filter_two,
        out_grad,
        *[jnp.asarray(t) for t in (fwd, bwd, dft, idft, twiddle)],
    )
    vmem = pl.BlockSpec(memory_space=pltpu.VMEM)
    flat = jax.ShapeDtypeStruct((rows, width), F32)
    output, token_grad, proj_grad, one, two = pl.pallas_call(
        finish_kernel,
        out_shape=(flat, flat, jax.ShapeDtypeStruct((3, depth // SEQ, width), F32), flat, flat),
        in_specs=[vmem] * 3,
        out_specs=(vmem,) * 5,
        name="finish",
    )(*arrived)
    return output, token_grad, proj_grad.transpose(1, 0, 2), one, two


def solution(mesh):
    in_specs = (
        P("seq", "chan"),
        P(None, None, "chan"),
        P("seq", "chan"),
        P("seq", "chan"),
        P("seq", "chan"),
    )
    out_specs = (
        P("seq", "chan"),
        P("seq", "chan"),
        P("seq", None, "chan"),
        P("seq", "chan"),
        P("seq", "chan"),
    )
    return jax.shard_map(shards, mesh=mesh, in_specs=in_specs, out_specs=out_specs, check_vma=False)
```
